32 devices in a mesh: gx: 4 (over y, x), gy: 8 (over z, core).
Axes of the slice: x: 2, y: 2, z: 4, core: 2. Of those that a mesh axis runs over, the one named last changes fastest.
Arguments:
- potential: float32 [96, 128, 128], P('gx', 'gy'), may hold values from -0.875 to 0.875
- density: float32 [96, 128, 128], P('gx', 'gy'), may hold values from 0.5 to 2
- correction: float32 [96, 128, 128], P('gx', 'gy'), may hold values from -6 to 6
Outputs:
- updated: float32 [96, 128, 128], P('gx', 'gy')
- residual: float32 [96, 128, 128], P('gx', 'gy')
The draws below stay inside these ranges and needn't reach their ends.
All inputs are finite; a program needn't handle non-finite values.
Results may differ from the reference program's by a relative error of at most 0.0003.
Values sent between devices are 32-bit elements; how exact they have to be, the bound alone decides.
A program may use at most 64 MiB of HBM per device.

```python
import jax
import jax.numpy as jnp

NZ = 128
FACTOR = 4
PRE = 2
POST = 2
COARSE_SWEEPS = 4
NX = 96
NY = 128


def draw_density(key, part):
    base = jax.random.uniform(key, (NX, NY, NZ), jnp.float32, 0.5, 2.0)
    return base


def block_levels(key, shape, shards, low, largest):
    level = 1.0
    for axis_at, shards_of in shards:
        steps = jax.random.uniform(jax.random.fold_in(jax.random.fold_in(key, 6), axis_at), (shards_of,), jnp.float32, low / len(shards), largest / len(shards))
        level = level * jnp.repeat(jnp.exp(steps), shape[axis_at] // shards_of).reshape((-1,) + (1,) * (len(shape) - 1 - axis_at))
    return level


def bell_draw(stream_key, extent, spread, bound, cuts=(), kind=jnp.bfloat16):
    array = spread * jax.random.normal(stream_key, extent, jnp.float32)
    if cuts:
        array = array * block_levels(stream_key, extent, cuts, -0.22, 0.18)
    return jnp.clip(array, -bound, bound).astype(kind)


def setup_inputs(seed: int = 0) -> dict:
    arg_keys = jax.random.split(jax.random.key(seed), 4)
    potential = bell_draw(arg_keys[0], (NX, NY, NZ), 0.06, 0.875, ((0, 4), (1, 8)), jnp.float32)
    density = draw_density(jax.random.fold_in(arg_keys[3], 71), 0)
    correction = bell_draw(arg_keys[2], (NX, NY, NZ), 0.5, 6.0, ((0, 4), (1, 8)), jnp.float32)
    return {"potential": potential, "density": density, "correction": correction}


screening = 0.002
damping = 0.6


def roller(values):
    def getter(shift_x, shift_y, shift_z):
        return jnp.roll(values, (-shift_x, -shift_y, -shift_z), axis=(0, 1, 2))
    return getter


def hessian(getter):
    centre = getter(0, 0, 0)

    def second(shift_x, shift_y, shift_z):
        return getter(shift_x, shift_y, shift_z) + getter(-shift_x, -shift_y, -shift_z) - 2.0 * centre

    def cross_term(ax_x, ax_y, ax_z, bx_x, bx_y, bx_z):
        plus_plus = getter(ax_x + bx_x, ax_y + bx_y, ax_z + bx_z)
        plus_minus = getter(ax_x - bx_x, ax_y - bx_y, ax_z - bx_z)
        minus_plus = getter(bx_x - ax_x, bx_y - ax_y, bx_z - ax_z)
        minus_minus = getter(-ax_x - bx_x, -ax_y - bx_y, -ax_z - bx_z)
        return 0.25 * (plus_plus - plus_minus - minus_plus + minus_minus)

    return (second(1, 0, 0), second(0, 1, 0), second(0, 0, 1),
            cross_term(1, 0, 0, 0, 1, 0), cross_term(1, 0, 0, 0, 0, 1), cross_term(0, 1, 0, 0, 0, 1))


def cofactors(hess):
    mat_xx = 1.0 + hess[0]
    mat_yy = 1.0 + hess[1]
    mat_zz = 1.0 + hess[2]
    mat_xy, mat_xz, mat_yz = hess[3], hess[4], hess[5]
    cof_xx = mat_yy * mat_zz - mat_yz * mat_yz
    cof_yy = mat_xx * mat_zz - mat_xz * mat_xz
    cof_zz = mat_xx * mat_yy - mat_xy * mat_xy
    cof_xy = mat_xz * mat_yz - mat_xy * mat_zz
    cof_xz = mat_xy * mat_yz - mat_xz * mat_yy
    cof_yz = mat_xy * mat_xz - mat_xx * mat_yz
    determinant = mat_xx * cof_xx + mat_xy * cof_xy + mat_xz * cof_xz
    return (cof_xx, cof_yy, cof_zz, cof_xy, cof_xz, cof_yz), determinant


def operate(getter, coeffs, spacing):
    centre = getter(0, 0, 0)
    terms = hessian(getter)
    summed = coeffs[0] * terms[0] + coeffs[1] * terms[1] + coeffs[2] * terms[2]
    summed = summed + 2.0 * (coeffs[3] * terms[3] + coeffs[4] * terms[4] + coeffs[5] * terms[5])
    return spacing * summed - screening * centre


def diagonal_of(coeffs, spacing):
    return -2.0 * spacing * (coeffs[0] + coeffs[1] + coeffs[2]) - screening


def relax(estimate, coeffs, diagonal, source, spacing):
    return estimate + damping * (source - operate(roller(estimate), coeffs, spacing)) / diagonal


def block_mean(values):
    size_x, size_y, size_z = values.shape
    shaped = values.reshape(size_x // FACTOR, FACTOR, size_y // FACTOR, FACTOR, size_z // FACTOR, FACTOR)
    return jnp.mean(shaped, axis=(1, 3, 5))


def spread_up(values):
    grown = jnp.repeat(values, FACTOR, axis=0)
    grown = jnp.repeat(grown, FACTOR, axis=1)
    return jnp.repeat(grown, FACTOR, axis=2)


def reference(potential, density, correction):
    coeffs, determinant = cofactors(hessian(roller(potential)))
    source = density - determinant
    diagonal = diagonal_of(coeffs, 1.0)
    estimate = correction
    for counter in range(PRE):
        estimate = relax(estimate, coeffs, diagonal, source, 1.0)
    fine_residual = source - operate(roller(estimate), coeffs, 1.0)
    coarse_source = block_mean(fine_residual)
    coarse_coeffs = tuple(block_mean(entry) for entry in coeffs)
    coarse_spacing = 1.0 / FACTOR ** 2
    coarse_diagonal = diagonal_of(coarse_coeffs, coarse_spacing)
    coarse = jnp.zeros(coarse_source.shape, jnp.float32)
    for counter in range(COARSE_SWEEPS):
        coarse = relax(coarse, coarse_coeffs, coarse_diagonal, coarse_source, coarse_spacing)
    estimate = estimate + spread_up(coarse)
    for counter in range(POST):
        estimate = relax(estimate, coeffs, diagonal, source, 1.0)
    residual = source - operate(roller(estimate), coeffs, 1.0)
    return estimate, residual
```

```python
import functools

import jax
import jax.numpy as jnp
from jax import lax
from jax.experimental import pallas as pl
from jax.experimental.pallas import tpu as pltpu
from jax.sharding import PartitionSpec as P

MESH = pl.DeviceIdType.MESH
SCREEN = 0.002
DAMP = 0.6
F32 = jnp.float32
NEIGHBOURS = [(-1, -1), (-1, 0), (-1, 1), (0, -1), (0, 1), (1, -1), (1, 0), (1, 1)]


def first_plane(ref, at):
    v = ref[at]
    rows = v.shape[0]
    zp = pltpu.roll(v, v.shape[1] - 1, 1)
    zm = pltpu.roll(v, 1, 1)
    yp = pltpu.roll(v, rows - 1, 0)
    ym = pltpu.roll(v, 1, 0)
    dz = zp - zm
    dyz = pltpu.roll(dz, rows - 1, 0) - pltpu.roll(dz, 1, 0)
    return v, dz, yp - ym, zp + zm, yp + ym, dyz


def walk(ref, low, high, emit, unroll=2):
    def step(at, carry):
        before, here = carry
        after = first_plane(ref, at + 1)
        emit(
            at,
            here[0],
            before[0] + after[0],
            here[4],
            here[3],
            after[2] - before[2],
            after[1] - before[1],
            here[5],
        )
        return here[:3], after

    start = (first_plane(ref, low - 1)[:3], first_plane(ref, low))
    lax.fori_loop(low, high, step, start, unroll=unroll)


def dot_exact(values, table):
    hi = values.astype(jnp.bfloat16)
    rest = values - hi.astype(F32)
    mid = rest.astype(jnp.bfloat16)
    lo = (rest - mid.astype(F32)).astype(jnp.bfloat16)
    n = values.shape[0]
    out = jnp.dot(jnp.concatenate([hi, mid, lo], axis=0), table, preferred_element_type=F32)
    return out[:n] + out[n : 2 * n] + out[2 * n :]


def kernel(
    gx_n, gy_n, p_in, d_in, c_in, up_out, res_out,
    pot, cor, den, coef, wgt, src, one, two, fin,
    msg_lo, msg_hi, got_lo, got_hi, est_lo, est_hi,
    pool_c, pool_s, co, cs, got_co, got_cs, wide, grown,
    in_sem, s1, r1, s2, r2, sc, rc, ss, rs,
):
    nx, ny, nz = p_in.shape
    x0, x1 = 4, 4 + nx
    gx = lax.axis_index("gx")
    gy = lax.axis_index("gy")

    def device(dx, dy):
        return (lax.rem(gx + dx + gx_n, gx_n), lax.rem(gy + dy + gy_n, gy_n))

    loads = []
    for k, (a, b) in enumerate(((p_in, pot), (c_in, cor), (d_in, den))):
        copy = pltpu.make_async_copy(a, b.at[x0:x1, 0:ny], in_sem.at[k])
        copy.start()
        loads.append(copy)
    barrier = pltpu.get_barrier_semaphore()
    for dx, dy in NEIGHBOURS:
        pl.semaphore_signal(barrier, inc=1, device_id=device(dx, dy), device_id_type=MESH)

    sub = lax.broadcasted_iota(jnp.int32, (8, nz), 0)
    wide[:, :, 14:16, :] = jnp.zeros((7, 3, 2, nz), F32)
    for f in range(6):
        pool_c[(f * 8 + 6) * ny : (f * 8 + 8) * ny, :] = jnp.zeros((2 * ny, nz), F32)
    pool_s[6 * ny : 8 * ny, :] = jnp.zeros((2 * ny, nz), F32)

    for copy in loads:
        copy.wait()

    def pack(x, _):
        top = ny - 8
        p, c, d = pot[x0 + x, top:ny], cor[x0 + x, top:ny], den[x0 + x, top:ny]
        msg_lo[x] = jnp.where(
            sub >= 5, p, jnp.where(sub >= 2, pltpu.roll(c, 5, 0), pltpu.roll(d, 2, 0))
        )
        p, c, d = pot[x0 + x, 0:8], cor[x0 + x, 0:8], den[x0 + x, 0:8]
        msg_hi[x] = jnp.where(
            sub < 3, p, jnp.where(sub < 6, pltpu.roll(c, 3, 0), pltpu.roll(d, 6, 0))
        )
        return 0

    lax.fori_loop(0, nx, pack, 0, unroll=4)
    pl.semaphore_wait(barrier, 8)

    def remote(a, b, send, recv, k, to):
        copy = pltpu.make_async_remote_copy(
            src_ref=a, dst_ref=b, send_sem=send.at[k], recv_sem=recv.at[k],
            device_id=to, device_id_type=MESH,
        )
        copy.start()
        return copy

    def y_sends(low, high, into_low, into_high, send, recv, k):
        out = []
        for dy, part, into in ((1, low, into_low), (-1, high, into_high)):
            out.append(remote(part(0, nx), into.at[x0:x1], send, recv, k, device(0, dy)))
            out.append(remote(part(0, 3), into.at[x1 : x1 + 3], send, recv, k + 1, device(-1, dy)))
            out.append(remote(part(nx - 3, nx), into.at[1:x0], send, recv, k + 2, device(1, dy)))
            k += 3
        return out

    round_1 = []
    k = 0
    for ref, width in ((pot, 3), (cor, 3), (den, 2)):
        round_1.append(remote(
            ref.at[x1 - width : x1, 0:ny], ref.at[x0 - width : x0, 0:ny], s1, r1, k, device(1, 0)))
        round_1.append(remote(
            ref.at[x0 : x0 + width, 0:ny], ref.at[x1 : x1 + width, 0:ny], s1, r1, k + 1, device(-1, 0)))
        k += 2
    round_1 += y_sends(
        lambda a, b: msg_lo.at[a:b], lambda a, b: msg_hi.at[a:b], got_lo, got_hi, s1, r1, k)

    rows_at = lax.broadcasted_iota(jnp.int32, (4 * nz, nz), 0)
    cols_at = lax.broadcasted_iota(jnp.int32, (4 * nz, nz), 1)
    group = nz // 4
    mean_table = jnp.where(
        (rows_at // nz) * group + (rows_at % nz) // 4 == cols_at, 1.0 / 64.0, 0.0
    ).astype(jnp.bfloat16)

    def pooled(ref, count):
        parts = []
        for y in range(4):
            total = ref[pl.ds(4 * y, count, stride=ny), :]
            for j in range(1, 4):
                total = total + ref[pl.ds(4 * y + j, count, stride=ny), :]
            parts.append(total)
        return dot_exact(jnp.concatenate(parts, axis=1), mean_table)

    for copy in round_1:
        copy.wait_recv()

    def unpack(at, _):
        lo, hi = got_lo[at], got_hi[at]
        pot[at, ny : ny + 8] = jnp.where(sub < 4, hi, lo)
        cor[at, ny : ny + 8] = jnp.where(sub < 4, pltpu.roll(hi, 5, 0), pltpu.roll(lo, 3, 0))
        den[at, ny : ny + 8] = jnp.where(sub < 4, pltpu.roll(hi, 2, 0), pltpu.roll(lo, 6, 0))
        return 0

    lax.fori_loop(1, x1 + 3, unpack, 0, unroll=3)

    def build(at, v, xs, ys, zs, dxy, dxz, dyz):
        twice = 2.0 * v
        xx, yy, zz = 1.0 + (xs - twice), 1.0 + (ys - twice), 1.0 + (zs - twice)
        xy, xz, yz = 0.25 * dxy, 0.25 * dxz, 0.25 * dyz
        cxx = yy * zz - yz * yz
        cyy = xx * zz - xz * xz
        czz = xx * yy - xy * xy
        cxy = xz * yz - xy * zz
        cxz = xy * yz - xz * yy
        cyz = xy * xz - xx * yz
        src[at] = den[at] - (xx * cxx + xy * cxy + xz * cxz)
        wgt[at] = DAMP / (-2.0 * (cxx + cyy + czz) - SCREEN)
        coef[0, at], coef[1, at], coef[2, at] = cxx, cyy, czz
        coef[3, at], coef[4, at], coef[5, at] = 0.5 * cxy, 0.5 * cxz, 0.5 * cyz

    walk(pot, x0 - 2, x1 + 2, build)

    def pool_coef(i, _):
        for f in range(6):
            total = coef[f, x0 + 4 * i, 0:ny]
            for j in range(1, 4):
                total = total + coef[f, x0 + 4 * i + j, 0:ny]
            pool_c[pl.ds(pl.multiple_of((f * 8 + i) * ny, 8), ny), :] = total
        return 0

    lax.fori_loop(0, nx // 4, pool_coef, 0)
    co[...] = pooled(pool_c, 48).reshape(6, 8, nz)
    coarse_c = [
        remote(co, got_co.at[7 - k], sc, rc, k, device(*NEIGHBOURS[k])) for k in range(8)
    ]

    def off_diagonal(at, xs, ys, zs, dxy, dxz, dyz):
        return (
            (coef[0, at] * xs + coef[1, at] * ys + coef[2, at] * zs)
            + (coef[3, at] * dxy + coef[4, at] * dxz + coef[5, at] * dyz)
        )

    def sweep(a, b, low, high):
        def emit(at, v, *terms):
            b[at] = (1.0 - DAMP) * v + wgt[at] * (src[at] - off_diagonal(at, *terms))

        walk(a, low, high, emit)

    def residual_at(at, v, *terms):
        n = ny
        cut = [t[0:n] for t in terms]
        c = [coef[f, at, 0:n] for f in range(6)]
        main = -2.0 * (c[0] + c[1] + c[2]) - SCREEN
        total = c[0] * cut[0] + c[1] * cut[1] + c[2] * cut[2]
        total = total + (c[3] * cut[3] + c[4] * cut[4] + c[5] * cut[5])
        return src[at, 0:n] - (total + main * v[0:n])

    sweep(cor, one, x0 - 2, x1 + 2)
    sweep(one, two, x0 - 1, x1 + 1)

    round_2 = [
        remote(two.at[x1 - 3 : x1, 0:ny], fin.at[1:x0, 0:ny], s2, r2, 0, device(1, 0)),
        remote(two.at[x0 : x0 + 3, 0:ny], fin.at[x1 : x1 + 3, 0:ny], s2, r2, 1, device(-1, 0)),
    ] + y_sends(
        lambda a, b: two.at[x0 + a : x0 + b, ny - 8 : ny],
        lambda a, b: two.at[x0 + a : x0 + b, 0:8],
        est_lo, est_hi, s2, r2, 2)

    def emit_first(at, v, *terms):
        res_out[at - x0] = residual_at(at, v, *terms)

    walk(two, x0, x1, emit_first)
    for i in range(nx // 4):
        pool_s[i * ny : (i + 1) * ny, :] = (
            (res_out[4 * i] + res_out[4 * i + 1]) + (res_out[4 * i + 2] + res_out[4 * i + 3])
        )
    cs[...] = pooled(pool_s, 8)
    coarse_s = [
        remote(cs, got_cs.at[7 - k], ss, rs, k, device(*NEIGHBOURS[k])) for k in range(8)
    ]

    def place(field, at_y, dx, value):
        if dx < 0:
            wide[field, at_y, 0:4, :] = value[2:6]
        elif dx == 0:
            wide[field, at_y, 4:10, :] = value[0:6]
        else:
            wide[field, at_y, 10:14, :] = value[0:4]

    for f in range(6):
        place(f, 1, 0, co[f])
    place(6, 1, 0, cs[...])
    for copy in coarse_c:
        copy.wait_recv()
    for k, (dx, dy) in enumerate(NEIGHBOURS):
        for f in range(6):
            place(f, dy + 1, dx, got_co[k, f])
    cc = [wide[f] for f in range(6)]
    spacing = 1.0 / 16.0
    coarse_w = DAMP / (-2.0 * spacing * (cc[0] + cc[1] + cc[2]) - SCREEN)
    cc = [spacing * c for c in cc]
    for copy in coarse_s:
        copy.wait_recv()
    for k, (dx, dy) in enumerate(NEIGHBOURS):
        place(6, dy + 1, dx, got_cs[k])
    coarse_b = wide[6]
    lane = lax.broadcasted_iota(jnp.int32, (3, 16, nz), 2)
    in_group = lane % group

    def y_up(v):
        r = pltpu.roll(v, nz - group, 2)
        return jnp.where(lane < nz - group, r, jnp.concatenate([r[1:], r[:1]], axis=0))

    def y_down(v):
        r = pltpu.roll(v, group, 2)
        return jnp.where(lane >= group, r, jnp.concatenate([r[2:], r[:2]], axis=0))

    value = coarse_w * coarse_b
    for _ in range(3):
        zp = jnp.where(in_group == group - 1, pltpu.roll(value, group - 1, 2), pltpu.roll(value, nz - 1, 2))
        zm = jnp.where(in_group == 0, pltpu.roll(value, nz - group + 1, 2), pltpu.roll(value, 1, 2))
        dz = zp - zm
        yp, ym = y_up(value), y_down(value)
        dy_ = yp - ym
        xs = pltpu.roll(value, 15, 1) + pltpu.roll(value, 1, 1)
        dxy = pltpu.roll(dy_, 15, 1) - pltpu.roll(dy_, 1, 1)
        dxz = pltpu.roll(dz, 15, 1) - pltpu.roll(dz, 1, 1)
        dyz = y_up(dz) - y_down(dz)
        total = cc[0] * xs + cc[1] * (yp + ym) + cc[2] * (zp + zm)
        total = total + (cc[3] * dxy + cc[4] * dxz + cc[5] * dyz)
        value = (1.0 - DAMP) * value + coarse_w * (coarse_b - total)

    rows_b = lax.broadcasted_iota(jnp.int32, (nz, nz), 0)
    cols_b = lax.broadcasted_iota(jnp.int32, (nz, nz), 1)
    for j, (blk, g) in enumerate(((0, 3), (1, 0), (1, 1), (1, 2), (1, 3), (2, 0))):
        table = jnp.where(rows_b == g * group + cols_b // 4, 1.0, 0.0).astype(jnp.bfloat16)
        grown[j] = dot_exact(value[blk], table)

    for copy in round_2:
        copy.wait_recv()

    def row(j, i):
        return jnp.broadcast_to(grown[j, 3 + i : 4 + i, :], (8, nz))

    for i in range(nx // 4 + 2):
        a0 = jnp.where(sub < 4, row(1, i), row(2, i))
        a1 = jnp.where(sub < 4, row(3, i), row(4, i))
        a2 = jnp.where(sub < 4, row(5, i), row(0, i))
        for at in range(4 * i, 4 * i + 4):
            if 1 <= at < x1 + 3:
                base = two if x0 <= at < x1 else fin
                fin[at, 0:8] = base[at, 0:8] + a0
                fin[at, 8:16] = base[at, 8:16] + a1
                fin[at, 16:24] = jnp.where(sub < 4, est_hi[at], est_lo[at]) + a2

    sweep(fin, one, x0 - 2, x1 + 2)
    for copy in round_2:
        copy.wait_send()
    sweep(one, two, x0 - 1, x1 + 1)

    def emit_last(at, v, *terms):
        up_out[at - x0] = v[0:ny]
        res_out[at - x0] = residual_at(at, v, *terms)

    walk(two, x0, x1, emit_last)
    for copy in round_1 + coarse_c + coarse_s:
        copy.wait_send()


def solution(mesh):
    gx_n, gy_n = mesh.shape["gx"], mesh.shape["gy"]

    def shards(potential, density, correction):
        nx, ny, nz = potential.shape
        fine = pltpu.VMEM((nx + 8, ny + 8, nz), F32)
        side = pltpu.VMEM((nx + 8, 8, nz), F32)
        dma = pltpu.SemaphoreType.DMA
        shape = jax.ShapeDtypeStruct(potential.shape, F32)
        return pl.pallas_call(
            functools.partial(kernel, gx_n, gy_n),
            out_shape=(shape, shape),
            in_specs=[pl.BlockSpec(memory_space=pl.ANY)] * 3,
            out_specs=[pl.BlockSpec(memory_space=pltpu.VMEM)] * 2,
            scratch_shapes=[
                fine, fine, fine,
                pltpu.VMEM((6, nx + 8, ny + 8, nz), F32),
                fine, fine, fine, fine, fine,
                pltpu.VMEM((nx, 8, nz), F32), pltpu.VMEM((nx, 8, nz), F32),
                side, side, side, side,
                pltpu.VMEM((48 * ny, nz), F32), pltpu.VMEM((8 * ny, nz), F32),
                pltpu.VMEM((6, 8, nz), F32), pltpu.VMEM((8, nz), F32),
                pltpu.VMEM((8, 6, 8, nz), F32), pltpu.VMEM((8, 8, nz), F32),
                pltpu.VMEM((7, 3, 16, nz), F32), pltpu.VMEM((6, 16, nz), F32),
                dma((3,)), dma((12,)), dma((12,)), dma((8,)), dma((8,)),
                dma((8,)), dma((8,)), dma((8,)), dma((8,)),
            ],
            compiler_params=pltpu.CompilerParams(
                collective_id=0, has_side_effects=True, vmem_limit_bytes=40 * 1024 * 1024
            ),
        )(potential, density, correction)

    placed = (P("gx", "gy", None),) * 3
    return jax.shard_map(
        shards, mesh=mesh, in_specs=placed,
        out_specs=(P("gx", "gy", None), P("gx", "gy", None)), check_vma=False,
    )
```

```python
import functools

import jax
import jax.numpy as jnp
from jax import lax
from jax.experimental import pallas as pl
from jax.experimental.pallas import tpu as pltpu
from jax.sharding import PartitionSpec as P

MESH = pl.DeviceIdType.MESH
SCREEN = 0.002
DAMP = 0.6
F32 = jnp.float32
NEIGHBOURS = [(-1, -1), (-1, 0), (-1, 1), (0, -1), (0, 1), (1, -1), (1, 0), (1, 1)]


def first_plane(ref, at):
    v = ref[at]
    rows = v.shape[0]
    zp = pltpu.roll(v, v.shape[1] - 1, 1)
    zm = pltpu.roll(v, 1, 1)
    yp = pltpu.roll(v, rows - 1, 0)
    ym = pltpu.roll(v, 1, 0)
    dz = zp - zm
    dyz = pltpu.roll(dz, rows - 1, 0) - pltpu.roll(dz, 1, 0)
    return v, dz, yp - ym, zp + zm, yp + ym, dyz


def walk(ref, low, high, emit):
    def step(at, carry):
        before, here = carry
        after = first_plane(ref, at + 1)
        emit(
            at,
            here[0],
            before[0] + after[0],
            here[4],
            here[3],
            after[2] - before[2],
            after[1] - before[1],
            here[5],
        )
        return here[:3], after

    start = (first_plane(ref, low - 1)[:3], first_plane(ref, low))
    lax.fori_loop(low, high, step, start, unroll=8 if (high - low) % 8 == 0 else 7)


def dot_exact(values, table):
    hi = values.astype(jnp.bfloat16)
    rest = values - hi.astype(F32)
    mid = rest.astype(jnp.bfloat16)
    lo = (rest - mid.astype(F32)).astype(jnp.bfloat16)
    n = values.shape[0]
    out = jnp.dot(jnp.concatenate([hi, mid, lo], axis=0), table, preferred_element_type=F32)
    return out[:n] + out[n : 2 * n] + out[2 * n :]


def kernel(
    gx_n, gy_n, p_in, d_in, c_in, up_out, res_out,
    pot, cor, den, coef, wgt, src, one, two, fin,
    msg_lo, msg_hi, got_lo, got_hi, out_lo, out_hi, est_lo, est_hi,
    pool_c, pool_s, co, co_lo, co_hi, cs, got_co, got_cox, got_cs, wide, grown,
    in_sem, s1, r1, s2, r2, sc, rc, ss, rs,
):
    nx, ny, nz = p_in.shape
    x0, x1 = 4, 4 + nx
    gx = lax.axis_index("gx")
    gy = lax.axis_index("gy")

    def device(dx, dy):
        return (lax.rem(gx + dx + gx_n, gx_n), lax.rem(gy + dy + gy_n, gy_n))

    barrier = pltpu.get_barrier_semaphore()
    for dx, dy in sorted(NEIGHBOURS, key=lambda d: -2 * abs(d[0]) - abs(d[1])):
        pl.semaphore_signal(barrier, inc=1, device_id=device(dx, dy), device_id_type=MESH)
    loads = []
    for k, (a, b) in enumerate(((p_in, pot), (c_in, cor), (d_in, den))):
        copy = pltpu.make_async_copy(a, b.at[x0:x1, 0:ny], in_sem.at[k])
        copy.start()
        loads.append(copy)
    sub = lax.broadcasted_iota(jnp.int32, (8, nz), 0)
    wide[:, :, 14:16, :] = jnp.zeros((7, 3, 2, nz), F32)
    for f in range(6):
        pool_c[(f * 8 + 6) * ny : (f * 8 + 8) * ny, :] = jnp.zeros((2 * ny, nz), F32)
    pool_s[6 * ny : 8 * ny, :] = jnp.zeros((2 * ny, nz), F32)

    for copy in loads:
        copy.wait()

    def pack(x, _):
        top = ny - 8
        p, c, d = pot[x0 + x, top:ny], cor[x0 + x, top:ny], den[x0 + x, top:ny]
        msg_lo[x] = jnp.where(
            sub >= 5, p, jnp.where(sub >= 2, pltpu.roll(c, 5, 0), pltpu.roll(d, 2, 0))
        )
        p, c, d = pot[x0 + x, 0:8], cor[x0 + x, 0:8], den[x0 + x, 0:8]
        msg_hi[x] = jnp.where(
            sub < 3, p, jnp.where(sub < 6, pltpu.roll(c, 3, 0), pltpu.roll(d, 6, 0))
        )
        return 0

    lax.fori_loop(0, nx, pack, 0, unroll=4)
    pl.semaphore_wait(barrier, 8)

    def remote(a, b, send, recv, k, to):
        copy = pltpu.make_async_remote_copy(
            src_ref=a, dst_ref=b, send_sem=send.at[k], recv_sem=recv.at[k],
            device_id=to, device_id_type=MESH,
        )
        copy.start()
        return copy

    def y_sends(low, high, into_low, into_high, send, recv, k, width, count, head):
        out = []
        tail = head + count
        for dy, part, into in ((1, low, into_low), (-1, high, into_high)):
            out.append(remote(
                part.at[0:width], into.at[tail : tail + width], send, recv, k, device(-1, dy)))
            out.append(remote(
                part.at[count - width : count], into.at[head - width : head],
                send, recv, k + 1, device(1, dy)))
            out.append(remote(part, into.at[head:tail], send, recv, k + 2, device(0, dy)))
            k += 3
        return out

    round_1 = []
    k = 0
    for ref, width in ((pot, 3), (cor, 3), (den, 2)):
        round_1.append(remote(
            ref.at[x1 - width : x1, 0:ny], ref.at[x0 - width : x0, 0:ny], s1, r1, k, device(1, 0)))
        round_1.append(remote(
            ref.at[x0 : x0 + width, 0:ny], ref.at[x1 : x1 + width, 0:ny], s1, r1, k + 1, device(-1, 0)))
        k += 2
    round_1 += y_sends(msg_lo, msg_hi, got_lo, got_hi, s1, r1, k, 3, nx, x0)

    rows_at = lax.broadcasted_iota(jnp.int32, (4 * nz, nz), 0)
    cols_at = lax.broadcasted_iota(jnp.int32, (4 * nz, nz), 1)
    group = nz // 4
    mean_table = jnp.where(
        (rows_at // nz) * group + (rows_at % nz) // 4 == cols_at, 1.0 / 64.0, 0.0
    ).astype(jnp.bfloat16)

    def pooled(ref, count):
        parts = []
        for y in range(4):
            total = ref[pl.ds(4 * y, count, stride=ny), :]
            for j in range(1, 4):
                total = total + ref[pl.ds(4 * y + j, count, stride=ny), :]
            parts.append(total)
        return dot_exact(jnp.concatenate(parts, axis=1), mean_table)

    for copy in round_1:
        copy.wait_recv()

    def unpack(at, _):
        lo, hi = got_lo[at], got_hi[at]
        pot[at, ny : ny + 8] = jnp.where(sub < 4, hi, lo)
        cor[at, ny : ny + 8] = jnp.where(sub < 4, pltpu.roll(hi, 5, 0), pltpu.roll(lo, 3, 0))
        den[at, ny : ny + 8] = jnp.where(sub < 4, pltpu.roll(hi, 2, 0), pltpu.roll(lo, 6, 0))
        return 0

    lax.fori_loop(1, x1 + 3, unpack, 0, unroll=3)

    def build(at, v, xs, ys, zs, dxy, dxz, dyz):
        twice = 2.0 * v
        xx, yy, zz = 1.0 + (xs - twice), 1.0 + (ys - twice), 1.0 + (zs - twice)
        xy, xz, yz = 0.25 * dxy, 0.25 * dxz, 0.25 * dyz
        cxx = yy * zz - yz * yz
        cyy = xx * zz - xz * xz
        czz = xx * yy - xy * xy
        cxy = xz * yz - xy * zz
        cxz = xy * yz - xz * yy
        cyz = xy * xz - xx * yz
        src[at] = den[at] - (xx * cxx + xy * cxy + xz * cxz)
        wgt[at] = DAMP / (-2.0 * (cxx + cyy + czz) - SCREEN)
        coef[0, at], coef[1, at], coef[2, at] = cxx, cyy, czz
        coef[3, at], coef[4, at], coef[5, at] = 0.5 * cxy, 0.5 * cxz, 0.5 * cyz

    walk(pot, x0 - 2, x1 + 2, build)

    def pool_coef(i, _):
        for f in range(6):
            total = coef[f, x0 + 4 * i, 0:ny]
            for j in range(1, 4):
                total = total + coef[f, x0 + 4 * i + j, 0:ny]
            pool_c[pl.ds(pl.multiple_of((f * 8 + i) * ny, 8), ny), :] = total
        return 0

    lax.fori_loop(0, nx // 4, pool_coef, 0)
    co[...] = pooled(pool_c, 48).reshape(6, 8, nz)
    for p in range(3):
        f, g = co[2 * p], co[2 * p + 1]
        co_lo[p] = jnp.where(sub < 4, pltpu.roll(f, 6, 0), pltpu.roll(g, 2, 0))
        co_hi[p] = jnp.where(sub < 4, f, pltpu.roll(g, 4, 0))
    coarse_c = []
    for k in (1, 6, 0, 2, 5, 7, 3, 4):
        dx = NEIGHBOURS[k][0]
        if dx == 0:
            a, b = co, got_co.at[(7 - k) - 3]
        else:
            a, b = (co_lo if dx > 0 else co_hi), got_cox.at[7 - k]
        coarse_c.append(remote(a, b, sc, rc, k, device(*NEIGHBOURS[k])))

    def off_diagonal(at, xs, ys, zs, dxy, dxz, dyz):
        return (
            (coef[0, at] * xs + coef[1, at] * ys + coef[2, at] * zs)
            + (coef[3, at] * dxy + coef[4, at] * dxz + coef[5, at] * dyz)
        )

    def sweep(a, b, low, high):
        def emit(at, v, *terms):
            b[at] = (1.0 - DAMP) * v + wgt[at] * (src[at] - off_diagonal(at, *terms))

        walk(a, low, high, emit)

    def residual_at(at, v, *terms):
        n = ny
        cut = [t[0:n] for t in terms]
        c = [coef[f, at, 0:n] for f in range(6)]
        main = -2.0 * (c[0] + c[1] + c[2]) - SCREEN
        total = c[0] * cut[0] + c[1] * cut[1] + c[2] * cut[2]
        total = total + (c[3] * cut[3] + c[4] * cut[4] + c[5] * cut[5])
        return src[at, 0:n] - (total + main * v[0:n])

    sweep(cor, one, x0 - 2, x1 + 2)
    sweep(one, two, x0 - 1, x1 + 1)

    round_2 = [
        remote(two.at[x1 - 3 : x1, 0:ny], fin.at[1:x0, 0:ny], s2, r2, 0, device(1, 0)),
        remote(two.at[x0 : x0 + 3, 0:ny], fin.at[x1 : x1 + 3, 0:ny], s2, r2, 1, device(-1, 0)),
    ]
    for q in range(nx // 2):
        a, b = x0 + 2 * q, x0 + 2 * q + 1
        out_lo[q] = jnp.where(sub < 4, pltpu.roll(two[a, ny - 8 : ny], 4, 0), two[b, ny - 8 : ny])
        out_hi[q] = jnp.where(sub < 4, two[a, 0:8], pltpu.roll(two[b, 0:8], 4, 0))
    round_2 += y_sends(out_lo, out_hi, est_lo, est_hi, s2, r2, 2, 2, nx // 2, x0 // 2)

    def emit_first(at, v, *terms):
        res_out[at - x0] = residual_at(at, v, *terms)

    walk(two, x0, x1, emit_first)
    for i in range(nx // 4):
        pool_s[i * ny : (i + 1) * ny, :] = (
            (res_out[4 * i] + res_out[4 * i + 1]) + (res_out[4 * i + 2] + res_out[4 * i + 3])
        )
    cs[...] = pooled(pool_s, 8)
    coarse_s = [
        remote(cs, got_cs.at[7 - k], ss, rs, k, device(*NEIGHBOURS[k])) for k in range(8)
    ]

    def place(field, at_y, dx, value):
        if dx < 0:
            wide[field, at_y, 0:4, :] = value[2:6]
        elif dx == 0:
            wide[field, at_y, 4:10, :] = value[0:6]
        else:
            wide[field, at_y, 10:14, :] = value[0:4]

    for f in range(6):
        place(f, 1, 0, co[f])
    place(6, 1, 0, cs[...])
    for copy in coarse_c:
        copy.wait_recv()
    for k, (dx, dy) in enumerate(NEIGHBOURS):
        for f in range(6):
            if dx == 0:
                place(f, dy + 1, 0, got_co[k - 3, f])
            else:
                row_at, part = (0 if dx < 0 else 10), 4 * (f % 2)
                wide[f, dy + 1, row_at : row_at + 4, :] = got_cox[k, f // 2, part : part + 4]
    cc = [wide[f] for f in range(6)]
    spacing = 1.0 / 16.0
    coarse_w = DAMP / (-2.0 * spacing * (cc[0] + cc[1] + cc[2]) - SCREEN)
    cc = [spacing * c for c in cc]
    for copy in coarse_s:
        copy.wait_recv()
    for k, (dx, dy) in enumerate(NEIGHBOURS):
        place(6, dy + 1, dx, got_cs[k])
    coarse_b = wide[6]
    lane = lax.broadcasted_iota(jnp.int32, (3, 16, nz), 2)
    in_group = lane % group

    def y_up(v):
        r = pltpu.roll(v, nz - group, 2)
        return jnp.where(lane < nz - group, r, jnp.concatenate([r[1:], r[:1]], axis=0))

    def y_down(v):
        r = pltpu.roll(v, group, 2)
        return jnp.where(lane >= group, r, jnp.concatenate([r[2:], r[:2]], axis=0))

    value = coarse_w * coarse_b
    for _ in range(3):
        zp = jnp.where(in_group == group - 1, pltpu.roll(value, group - 1, 2), pltpu.roll(value, nz - 1, 2))
        zm = jnp.where(in_group == 0, pltpu.roll(value, nz - group + 1, 2), pltpu.roll(value, 1, 2))
        dz = zp - zm
        yp, ym = y_up(value), y_down(value)
        dy_ = yp - ym
        xs = pltpu.roll(value, 15, 1) + pltpu.roll(value, 1, 1)
        dxy = pltpu.roll(dy_, 15, 1) - pltpu.roll(dy_, 1, 1)
        dxz = pltpu.roll(dz, 15, 1) - pltpu.roll(dz, 1, 1)
        dyz = y_up(dz) - y_down(dz)
        total = cc[0] * xs + cc[1] * (yp + ym) + cc[2] * (zp + zm)
        total = total + (cc[3] * dxy + cc[4] * dxz + cc[5] * dyz)
        value = (1.0 - DAMP) * value + coarse_w * (coarse_b - total)

    rows_b = lax.broadcasted_iota(jnp.int32, (nz, nz), 0)
    cols_b = lax.broadcasted_iota(jnp.int32, (nz, nz), 1)
    for j, (blk, g) in enumerate(((0, 3), (1, 0), (1, 1), (1, 2), (1, 3), (2, 0))):
        table = jnp.where(rows_b == g * group + cols_b // 4, 1.0, 0.0).astype(jnp.bfloat16)
        grown[j] = dot_exact(value[blk], table)

    for copy in round_2:
        copy.wait_recv()

    def row(j, i):
        return jnp.broadcast_to(grown[j, 3 + i : 4 + i, :], (8, nz))

    for i in range(nx // 4 + 2):
        a0 = jnp.where(sub < 4, row(1, i), row(2, i))
        a1 = jnp.where(sub < 4, row(3, i), row(4, i))
        a2 = jnp.where(sub < 4, row(5, i), row(0, i))
        for at in range(4 * i, 4 * i + 4):
            if 1 <= at < x1 + 3:
                base = two if x0 <= at < x1 else fin
                fin[at, 0:8] = base[at, 0:8] + a0
                fin[at, 8:16] = base[at, 8:16] + a1
                lo, hi = est_lo[at // 2], est_hi[at // 2]
                if at % 2 == 0:
                    lo = pltpu.roll(lo, 4, 0)
                else:
                    hi = pltpu.roll(hi, 4, 0)
                fin[at, ny : ny + 8] = jnp.where(sub < 4, hi, lo) + a2

    sweep(fin, one, x0 - 2, x1 + 2)
    for copy in round_2:
        copy.wait_send()
    sweep(one, two, x0 - 1, x1 + 1)

    def emit_last(at, v, *terms):
        up_out[at - x0] = v[0:ny]
        res_out[at - x0] = residual_at(at, v, *terms)

    walk(two, x0, x1, emit_last)
    for copy in round_1 + coarse_c + coarse_s:
        copy.wait_send()


def solution(mesh):
    gx_n, gy_n = mesh.shape["gx"], mesh.shape["gy"]

    def shards(potential, density, correction):
        nx, ny, nz = potential.shape
        fine = pltpu.VMEM((nx + 8, ny + 8, nz), F32)
        side = pltpu.VMEM((nx + 8, 8, nz), F32)
        half_out = pltpu.VMEM((nx // 2, 8, nz), F32)
        half = pltpu.VMEM((nx // 2 + 4, 8, nz), F32)
        dma = pltpu.SemaphoreType.DMA
        shape = jax.ShapeDtypeStruct(potential.shape, F32)
        return pl.pallas_call(
            functools.partial(kernel, gx_n, gy_n),
            out_shape=(shape, shape),
            in_specs=[pl.BlockSpec(memory_space=pl.ANY)] * 3,
            out_specs=[pl.BlockSpec(memory_space=pltpu.VMEM)] * 2,
            scratch_shapes=[
                fine, fine, fine,
                pltpu.VMEM((6, nx + 8, ny + 8, nz), F32),
                fine, fine, fine, fine, fine,
                pltpu.VMEM((nx, 8, nz), F32), pltpu.VMEM((nx, 8, nz), F32),
                side, side, half_out, half_out, half, half,
                pltpu.VMEM((48 * ny, nz), F32), pltpu.VMEM((8 * ny, nz), F32),
                pltpu.VMEM((6, 8, nz), F32), pltpu.VMEM((3, 8, nz), F32), pltpu.VMEM((3, 8, nz), F32),
                pltpu.VMEM((8, nz), F32),
                pltpu.VMEM((2, 6, 8, nz), F32), pltpu.VMEM((8, 3, 8, nz), F32), pltpu.VMEM((8, 8, nz), F32),
                pltpu.VMEM((7, 3, 16, nz), F32), pltpu.VMEM((6, 16, nz), F32),
                dma((3,)), dma((12,)), dma((12,)), dma((8,)), dma((8,)),
                dma((8,)), dma((8,)), dma((8,)), dma((8,)),
            ],
            compiler_params=pltpu.CompilerParams(
                collective_id=0, has_side_effects=True, vmem_limit_bytes=40 * 1024 * 1024
            ),
        )(*[
            pltpu.with_memory_space_constraint(v, pltpu.HBM) for v in (potential, density, correction)
        ])

    placed = (P("gx", "gy", None),) * 3
    return jax.shard_map(
        shards, mesh=mesh, in_specs=placed,
        out_specs=(P("gx", "gy", None), P("gx", "gy", None)), check_vma=False,
    )
```

```python
import functools

import jax
import jax.numpy as jnp
from jax import lax
from jax.experimental import pallas as pl
from jax.experimental.pallas import tpu as pltpu
from jax.sharding import PartitionSpec as P

MESH = pl.DeviceIdType.MESH
SCREEN = 0.002
DAMP = 0.6
UNROLL = {3: 3, 4: 4, 20: 10, 22: 11, 24: 8}
F32 = jnp.float32
BESIDE = [(-1, 0), (1, 0), (0, -1), (0, 1)]
NEIGHBOURS = [(-1, -1), (-1, 0), (-1, 1), (0, -1), (0, 1), (1, -1), (1, 0), (1, 1)]


def first_plane(ref, at):
    v = ref[at]
    rows = v.shape[0]
    zp = pltpu.roll(v, v.shape[1] - 1, 1)
    zm = pltpu.roll(v, 1, 1)
    yp = pltpu.roll(v, rows - 1, 0)
    ym = pltpu.roll(v, 1, 0)
    dz = zp - zm
    dyz = pltpu.roll(dz, rows - 1, 0) - pltpu.roll(dz, 1, 0)
    return v, dz, yp - ym, zp + zm, yp + ym, dyz


def walk(ref, low, high, emit):
    def step(at, carry):
        before, here = carry
        after = first_plane(ref, at + 1)
        emit(
            at,
            here[0],
            before[0] + after[0],
            here[4],
            here[3],
            after[2] - before[2],
            after[1] - before[1],
            here[5],
        )
        return here[:3], after

    start = (first_plane(ref, low - 1)[:3], first_plane(ref, low))
    lax.fori_loop(low, high, step, start, unroll=UNROLL.get(high - low, 7))


def dot_exact(values, table):
    hi = values.astype(jnp.bfloat16)
    rest = values - hi.astype(F32)
    mid = rest.astype(jnp.bfloat16)
    lo = (rest - mid.astype(F32)).astype(jnp.bfloat16)
    n = values.shape[0]
    out = jnp.dot(jnp.concatenate([hi, mid, lo], axis=0), table, preferred_element_type=F32)
    return out[:n] + out[n : 2 * n] + out[2 * n :]


def kernel(
    gx_n, gy_n, p_in, d_in, c_in, up_out, res_out,
    pot, cor, den, coef, wgt, src, one, two, fin,
    msg_lo, msg_hi, got_lo, got_hi, out_lo, out_hi, est_lo, est_hi,
    pool_c, pool_s, co, co_lo, co_hi, cs, got_co, got_cox, got_cs, wide, grown,
    in_sem, s1, r1, s2, r2, sc, rc, ss, rs,
):
    nx, ny, nz = p_in.shape
    x0, x1 = 4, 4 + nx
    gx = lax.axis_index("gx")
    gy = lax.axis_index("gy")

    def device(dx, dy):
        return (lax.rem(gx + dx + gx_n, gx_n), lax.rem(gy + dy + gy_n, gy_n))

    barrier = pltpu.get_barrier_semaphore()
    for dx, dy in BESIDE:
        pl.semaphore_signal(barrier, inc=1, device_id=device(dx, dy), device_id_type=MESH)
    loads = []
    for k, (a, b) in enumerate(((p_in, pot), (c_in, cor), (d_in, den))):
        copy = pltpu.make_async_copy(a, b.at[x0:x1, 0:ny], in_sem.at[k])
        copy.start()
        loads.append(copy)
    sub = lax.broadcasted_iota(jnp.int32, (8, nz), 0)
    wide[:, :, 14:16, :] = jnp.zeros((7, 3, 2, nz), F32)
    for f in range(6):
        pool_c[(f * 8 + 6) * ny : (f * 8 + 8) * ny, :] = jnp.zeros((2 * ny, nz), F32)
    pool_s[6 * ny : 8 * ny, :] = jnp.zeros((2 * ny, nz), F32)

    for copy in loads:
        copy.wait()

    def pack(x, _):
        top = ny - 8
        p, c, d = pot[x0 + x, top:ny], cor[x0 + x, top:ny], den[x0 + x, top:ny]
        msg_lo[x] = jnp.where(
            sub >= 5, p, jnp.where(sub >= 2, pltpu.roll(c, 5, 0), pltpu.roll(d, 2, 0))
        )
        p, c, d = pot[x0 + x, 0:8], cor[x0 + x, 0:8], den[x0 + x, 0:8]
        msg_hi[x] = jnp.where(
            sub < 3, p, jnp.where(sub < 6, pltpu.roll(c, 3, 0), pltpu.roll(d, 6, 0))
        )
        return 0

    lax.fori_loop(0, nx, pack, 0, unroll=4)
    pl.semaphore_wait(barrier, 4)

    def remote(a, b, send, recv, k, to):
        copy = pltpu.make_async_remote_copy(
            src_ref=a, dst_ref=b, send_sem=send.at[k], recv_sem=recv.at[k],
            device_id=to, device_id_type=MESH,
        )
        copy.start()
        return copy

    def y_sends(low, high, into_low, into_high, send, recv, k, width, count, head):
        out = []
        tail = head + count
        for dy, part, into in ((1, low, into_low), (-1, high, into_high)):
            out.append(remote(
                part.at[0:width], into.at[tail : tail + width], send, recv, k, device(-1, dy)))
            out.append(remote(
                part.at[count - width : count], into.at[head - width : head],
                send, recv, k + 1, device(1, dy)))
            out.append(remote(part, into.at[head:tail], send, recv, k + 2, device(0, dy)))
            k += 3
        return out

    got = ((got_lo, msg_lo, 1), (got_hi, msg_hi, -1))
    beside_y = [
        remote(msg, into.at[x0:x1], s1, r1, k, device(0, dy)) for k, (into, msg, dy) in enumerate(got)
    ]
    beside_x = []
    k = 2
    for ref, width in ((pot, 3), (cor, 3), (den, 2)):
        beside_x.append(remote(
            ref.at[x1 - width : x1, 0:ny], ref.at[x0 - width : x0, 0:ny], s1, r1, k, device(1, 0)))
        beside_x.append(remote(
            ref.at[x0 : x0 + width, 0:ny], ref.at[x1 : x1 + width, 0:ny], s1, r1, k + 1, device(-1, 0)))
        k += 2

    rows_at = lax.broadcasted_iota(jnp.int32, (4 * nz, nz), 0)
    cols_at = lax.broadcasted_iota(jnp.int32, (4 * nz, nz), 1)
    group = nz // 4
    mean_table = jnp.where(
        (rows_at // nz) * group + (rows_at % nz) // 4 == cols_at, 1.0 / 64.0, 0.0
    ).astype(jnp.bfloat16)

    def pooled(ref, count):
        parts = []
        for y in range(4):
            total = ref[pl.ds(4 * y, count, stride=ny), :]
            for j in range(1, 4):
                total = total + ref[pl.ds(4 * y + j, count, stride=ny), :]
            parts.append(total)
        return dot_exact(jnp.concatenate(parts, axis=1), mean_table)

    for copy in beside_y:
        copy.wait_recv()
    for into in (got_lo, got_hi):
        beside_x.append(remote(
            into.at[x1 - 3 : x1], into.at[1:x0], s1, r1, k, device(1, 0)))
        beside_x.append(remote(
            into.at[x0 : x0 + 3], into.at[x1 : x1 + 3], s1, r1, k + 1, device(-1, 0)))
        k += 2
    round_1 = beside_y + beside_x

    def unpack(at, _):
        lo, hi = got_lo[at], got_hi[at]
        pot[at, ny : ny + 8] = jnp.where(sub < 4, hi, lo)
        cor[at, ny : ny + 8] = jnp.where(sub < 4, pltpu.roll(hi, 5, 0), pltpu.roll(lo, 3, 0))
        den[at, ny : ny + 8] = jnp.where(sub < 4, pltpu.roll(hi, 2, 0), pltpu.roll(lo, 6, 0))
        return 0

    lax.fori_loop(x0, x1, unpack, 0, unroll=4)

    def build(at, v, xs, ys, zs, dxy, dxz, dyz):
        twice = 2.0 * v
        xx, yy, zz = 1.0 + (xs - twice), 1.0 + (ys - twice), 1.0 + (zs - twice)
        xy, xz, yz = 0.25 * dxy, 0.25 * dxz, 0.25 * dyz
        cxx = yy * zz - yz * yz
        cyy = xx * zz - xz * xz
        czz = xx * yy - xy * xy
        cxy = xz * yz - xy * zz
        cxz = xy * yz - xz * yy
        cyz = xy * xz - xx * yz
        src[at] = den[at] - (xx * cxx + xy * cxy + xz * cxz)
        wgt[at] = DAMP / (-2.0 * (cxx + cyy + czz) - SCREEN)
        coef[0, at], coef[1, at], coef[2, at] = cxx, cyy, czz
        coef[3, at], coef[4, at], coef[5, at] = 0.5 * cxy, 0.5 * cxz, 0.5 * cyz

    def off_diagonal(at, xs, ys, zs, dxy, dxz, dyz):
        return (
            (coef[0, at] * xs + coef[1, at] * ys + coef[2, at] * zs)
            + (coef[3, at] * dxy + coef[4, at] * dxz + coef[5, at] * dyz)
        )

    def sweep(a, b, low, high):
        def emit(at, v, *terms):
            b[at] = (1.0 - DAMP) * v + wgt[at] * (src[at] - off_diagonal(at, *terms))

        walk(a, low, high, emit)

    walk(pot, x0 + 1, x1 - 1, build)
    sweep(cor, one, x0 + 2, x1 - 2)
    for copy in beside_x:
        copy.wait_recv()
    lax.fori_loop(1, x0, unpack, 0, unroll=3)
    lax.fori_loop(x1, x1 + 3, unpack, 0, unroll=3)
    walk(pot, x0 - 2, x0 + 1, build)
    walk(pot, x1 - 1, x1 + 2, build)

    def pool_coef(i, _):
        for f in range(6):
            total = coef[f, x0 + 4 * i, 0:ny]
            for j in range(1, 4):
                total = total + coef[f, x0 + 4 * i + j, 0:ny]
            pool_c[pl.ds(pl.multiple_of((f * 8 + i) * ny, 8), ny), :] = total
        return 0

    lax.fori_loop(0, nx // 4, pool_coef, 0)
    co[...] = pooled(pool_c, 48).reshape(6, 8, nz)
    for p in range(3):
        f, g = co[2 * p], co[2 * p + 1]
        co_lo[p] = jnp.where(sub < 4, pltpu.roll(f, 6, 0), pltpu.roll(g, 2, 0))
        co_hi[p] = jnp.where(sub < 4, f, pltpu.roll(g, 4, 0))
    coarse_c = []
    for k in (1, 6, 0, 2, 5, 7, 3, 4):
        dx = NEIGHBOURS[k][0]
        if dx == 0:
            a, b = co, got_co.at[(7 - k) - 3]
        else:
            a, b = (co_lo if dx > 0 else co_hi), got_cox.at[7 - k]
        coarse_c.append(remote(a, b, sc, rc, k, device(*NEIGHBOURS[k])))

    def residual_at(at, v, *terms):
        n = ny
        cut = [t[0:n] for t in terms]
        c = [coef[f, at, 0:n] for f in range(6)]
        main = -2.0 * (c[0] + c[1] + c[2]) - SCREEN
        total = c[0] * cut[0] + c[1] * cut[1] + c[2] * cut[2]
        total = total + (c[3] * cut[3] + c[4] * cut[4] + c[5] * cut[5])
        return src[at, 0:n] - (total + main * v[0:n])

    sweep(cor, one, x0 - 2, x0 + 2)
    sweep(cor, one, x1 - 2, x1 + 2)
    sweep(one, two, x0 - 1, x1 + 1)

    round_2 = [
        remote(two.at[x1 - 3 : x1, 0:ny], fin.at[1:x0, 0:ny], s2, r2, 0, device(1, 0)),
        remote(two.at[x0 : x0 + 3, 0:ny], fin.at[x1 : x1 + 3, 0:ny], s2, r2, 1, device(-1, 0)),
    ]
    for q in range(nx // 2):
        a, b = x0 + 2 * q, x0 + 2 * q + 1
        out_lo[q] = jnp.where(sub < 4, pltpu.roll(two[a, ny - 8 : ny], 4, 0), two[b, ny - 8 : ny])
        out_hi[q] = jnp.where(sub < 4, two[a, 0:8], pltpu.roll(two[b, 0:8], 4, 0))
    round_2 += y_sends(out_lo, out_hi, est_lo, est_hi, s2, r2, 2, 2, nx // 2, x0 // 2)

    def emit_first(at, v, *terms):
        res_out[at - x0] = residual_at(at, v, *terms)

    walk(two, x0, x1, emit_first)
    for i in range(nx // 4):
        pool_s[i * ny : (i + 1) * ny, :] = (
            (res_out[4 * i] + res_out[4 * i + 1]) + (res_out[4 * i + 2] + res_out[4 * i + 3])
        )
    cs[...] = pooled(pool_s, 8)
    coarse_s = [
        remote(cs, got_cs.at[7 - k], ss, rs, k, device(*NEIGHBOURS[k])) for k in range(8)
    ]

    def place(field, at_y, dx, value):
        if dx < 0:
            wide[field, at_y, 0:4, :] = value[2:6]
        elif dx == 0:
            wide[field, at_y, 4:10, :] = value[0:6]
        else:
            wide[field, at_y, 10:14, :] = value[0:4]

    for f in range(6):
        place(f, 1, 0, co[f])
    place(6, 1, 0, cs[...])
    for copy in coarse_c:
        copy.wait_recv()
    for k, (dx, dy) in enumerate(NEIGHBOURS):
        for f in range(6):
            if dx == 0:
                place(f, dy + 1, 0, got_co[k - 3, f])
            else:
                row_at, part = (0 if dx < 0 else 10), 4 * (f % 2)
                wide[f, dy + 1, row_at : row_at + 4, :] = got_cox[k, f // 2, part : part + 4]
    cc = [wide[f] for f in range(6)]
    spacing = 1.0 / 16.0
    coarse_w = DAMP / (-2.0 * spacing * (cc[0] + cc[1] + cc[2]) - SCREEN)
    cc = [spacing * c for c in cc]
    for copy in coarse_s:
        copy.wait_recv()
    for k, (dx, dy) in enumerate(NEIGHBOURS):
        place(6, dy + 1, dx, got_cs[k])
    coarse_b = wide[6]
    lane = lax.broadcasted_iota(jnp.int32, (3, 16, nz), 2)
    in_group = lane % group

    def y_up(v):
        r = pltpu.roll(v, nz - group, 2)
        return jnp.where(lane < nz - group, r, jnp.concatenate([r[1:], r[:1]], axis=0))

    def y_down(v):
        r = pltpu.roll(v, group, 2)
        return jnp.where(lane >= group, r, jnp.concatenate([r[2:], r[:2]], axis=0))

    value = coarse_w * coarse_b
    for _ in range(3):
        zp = jnp.where(in_group == group - 1, pltpu.roll(value, group - 1, 2), pltpu.roll(value, nz - 1, 2))
        zm = jnp.where(in_group == 0, pltpu.roll(value, nz - group + 1, 2), pltpu.roll(value, 1, 2))
        dz = zp - zm
        yp, ym = y_up(value), y_down(value)
        dy_ = yp - ym
        xs = pltpu.roll(value, 15, 1) + pltpu.roll(value, 1, 1)
        dxy = pltpu.roll(dy_, 15, 1) - pltpu.roll(dy_, 1, 1)
        dxz = pltpu.roll(dz, 15, 1) - pltpu.roll(dz, 1, 1)
        dyz = y_up(dz) - y_down(dz)
        total = cc[0] * xs + cc[1] * (yp + ym) + cc[2] * (zp + zm)
        total = total + (cc[3] * dxy + cc[4] * dxz + cc[5] * dyz)
        value = (1.0 - DAMP) * value + coarse_w * (coarse_b - total)

    rows_b = lax.broadcasted_iota(jnp.int32, (nz, nz), 0)
    cols_b = lax.broadcasted_iota(jnp.int32, (nz, nz), 1)
    for j, (blk, g) in enumerate(((0, 3), (1, 0), (1, 1), (1, 2), (1, 3), (2, 0))):
        table = jnp.where(rows_b == g * group + cols_b // 4, 1.0, 0.0).astype(jnp.bfloat16)
        grown[j] = dot_exact(value[blk], table)

    for copy in round_2:
        copy.wait_recv()

    def row(j, i):
        return jnp.broadcast_to(grown[j, 3 + i : 4 + i, :], (8, nz))

    for i in range(nx // 4 + 2):
        a0 = jnp.where(sub < 4, row(1, i), row(2, i))
        a1 = jnp.where(sub < 4, row(3, i), row(4, i))
        a2 = jnp.where(sub < 4, row(5, i), row(0, i))
        for at in range(4 * i, 4 * i + 4):
            if 1 <= at < x1 + 3:
                base = two if x0 <= at < x1 else fin
                fin[at, 0:8] = base[at, 0:8] + a0
                fin[at, 8:16] = base[at, 8:16] + a1
                lo, hi = est_lo[at // 2], est_hi[at // 2]
                if at % 2 == 0:
                    lo = pltpu.roll(lo, 4, 0)
                else:
                    hi = pltpu.roll(hi, 4, 0)
                fin[at, ny : ny + 8] = jnp.where(sub < 4, hi, lo) + a2

    sweep(fin, one, x0 - 2, x1 + 2)
    for copy in round_2:
        copy.wait_send()
    sweep(one, two, x0 - 1, x1 + 1)

    def emit_last(at, v, *terms):
        up_out[at - x0] = v[0:ny]
        res_out[at - x0] = residual_at(at, v, *terms)

    walk(two, x0, x1, emit_last)
    for copy in round_1 + coarse_c + coarse_s:
        copy.wait_send()


def solution(mesh):
    gx_n, gy_n = mesh.shape["gx"], mesh.shape["gy"]

    def shards(potential, density, correction):
        nx, ny, nz = potential.shape
        fine = pltpu.VMEM((nx + 8, ny + 8, nz), F32)
        side = pltpu.VMEM((nx + 8, 8, nz), F32)
        half_out = pltpu.VMEM((nx // 2, 8, nz), F32)
        half = pltpu.VMEM((nx // 2 + 4, 8, nz), F32)
        dma = pltpu.SemaphoreType.DMA
        shape = jax.ShapeDtypeStruct(potential.shape, F32)
        return pl.pallas_call(
            functools.partial(kernel, gx_n, gy_n),
            out_shape=(shape, shape),
            in_specs=[pl.BlockSpec(memory_space=pl.ANY)] * 3,
            out_specs=[pl.BlockSpec(memory_space=pltpu.VMEM)] * 2,
            scratch_shapes=[
                fine, fine, fine,
                pltpu.VMEM((6, nx + 8, ny + 8, nz), F32),
                fine, fine, fine, fine, fine,
                pltpu.VMEM((nx, 8, nz), F32), pltpu.VMEM((nx, 8, nz), F32),
                side, side, half_out, half_out, half, half,
                pltpu.VMEM((48 * ny, nz), F32), pltpu.VMEM((8 * ny, nz), F32),
                pltpu.VMEM((6, 8, nz), F32), pltpu.VMEM((3, 8, nz), F32), pltpu.VMEM((3, 8, nz), F32),
                pltpu.VMEM((8, nz), F32),
                pltpu.VMEM((2, 6, 8, nz), F32), pltpu.VMEM((8, 3, 8, nz), F32), pltpu.VMEM((8, 8, nz), F32),
                pltpu.VMEM((7, 3, 16, nz), F32), pltpu.VMEM((6, 16, nz), F32),
                dma((3,)), dma((12,)), dma((12,)), dma((8,)), dma((8,)),
                dma((8,)), dma((8,)), dma((8,)), dma((8,)),
            ],
            compiler_params=pltpu.CompilerParams(
                collective_id=0, has_side_effects=True, vmem_limit_bytes=40 * 1024 * 1024
            ),
        )(*[
            pltpu.with_memory_space_constraint(v, pltpu.HBM) for v in (potential, density, correction)
        ])

    placed = (P("gx", "gy", None),) * 3
    return jax.shard_map(
        shards, mesh=mesh, in_specs=placed,
        out_specs=(P("gx", "gy", None), P("gx", "gy", None)), check_vma=False,
    )
```

```python
import functools

import jax
import jax.numpy as jnp
from jax import lax
from jax.experimental import pallas as pl
from jax.experimental.pallas import tpu as pltpu
from jax.sharding import PartitionSpec as P

MESH = pl.DeviceIdType.MESH
SCREEN = 0.002
DAMP = 0.6
UNROLL = {3: 3, 4: 4, 20: 10, 22: 11, 24: 12, 26: 13, 28: 14}
F32 = jnp.float32
BESIDE = [(-1, 0), (1, 0), (0, -1), (0, 1)]
NEIGHBOURS = [(-1, -1), (-1, 0), (-1, 1), (0, -1), (0, 1), (1, -1), (1, 0), (1, 1)]


def first_plane(ref, at):
    v = ref[at]
    rows = v.shape[0]
    zp = pltpu.roll(v, v.shape[1] - 1, 1)
    zm = pltpu.roll(v, 1, 1)
    yp = pltpu.roll(v, rows - 1, 0)
    ym = pltpu.roll(v, 1, 0)
    dz = zp - zm
    dyz = pltpu.roll(dz, rows - 1, 0) - pltpu.roll(dz, 1, 0)
    return v, dz, yp - ym, zp + zm, yp + ym, dyz


def walk(ref, low, high, emit):
    def step(at, carry):
        before, here = carry
        after = first_plane(ref, at + 1)
        emit(
            at,
            here[0],
            before[0] + after[0],
            here[4],
            here[3],
            after[2] - before[2],
            after[1] - before[1],
            here[5],
        )
        return here[:3], after

    start = (first_plane(ref, low - 1)[:3], first_plane(ref, low))
    lax.fori_loop(low, high, step, start, unroll=UNROLL.get(high - low, 7))


def dot_exact(values, table):
    hi = values.astype(jnp.bfloat16)
    rest = values - hi.astype(F32)
    mid = rest.astype(jnp.bfloat16)
    lo = (rest - mid.astype(F32)).astype(jnp.bfloat16)
    n = values.shape[0]
    out = jnp.dot(jnp.concatenate([hi, mid, lo], axis=0), table, preferred_element_type=F32)
    return out[:n] + out[n : 2 * n] + out[2 * n :]


def kernel(
    gx_n, gy_n, p_in, d_in, c_in, up_out, res_out,
    pot, cor, den, coef, wgt, src, one, two, fin,
    msg_lo, msg_hi, got_lo, got_hi, out_lo, out_hi, est_lo, est_hi,
    pool_c, pool_s, co, co_lo, co_hi, cs, got_co, got_cox, got_cs, wide, grown, back,
    in_sem, s1, r1, s2, r2, sc, rc, ss, rs,
):
    nx, ny, nz = p_in.shape
    x0, x1 = 4, 4 + nx
    gx = lax.axis_index("gx")
    gy = lax.axis_index("gy")

    def device(dx, dy):
        return (lax.rem(gx + dx + gx_n, gx_n), lax.rem(gy + dy + gy_n, gy_n))

    barrier = pltpu.get_barrier_semaphore()
    for dx, dy in BESIDE:
        pl.semaphore_signal(barrier, inc=1, device_id=device(dx, dy), device_id_type=MESH)
    loads = []
    for k, (a, b) in enumerate(((p_in, pot), (c_in, cor), (d_in, den))):
        copy = pltpu.make_async_copy(a, b.at[x0:x1, 0:ny], in_sem.at[k])
        copy.start()
        loads.append(copy)
    sub = lax.broadcasted_iota(jnp.int32, (8, nz), 0)
    wide[:, :, 14:16, :] = jnp.zeros((7, 3, 2, nz), F32)
    for f in range(6):
        pool_c[(f * 8 + 6) * ny : (f * 8 + 8) * ny, :] = jnp.zeros((2 * ny, nz), F32)
    pool_s[6 * ny : 8 * ny, :] = jnp.zeros((2 * ny, nz), F32)

    for copy in loads:
        copy.wait()

    def pack(x, _):
        top = ny - 8
        p, c, d = pot[x0 + x, top:ny], cor[x0 + x, top:ny], den[x0 + x, top:ny]
        msg_lo[x] = jnp.where(
            sub >= 5, p, jnp.where(sub >= 2, pltpu.roll(c, 5, 0), pltpu.roll(d, 2, 0))
        )
        p, c, d = pot[x0 + x, 0:8], cor[x0 + x, 0:8], den[x0 + x, 0:8]
        msg_hi[x] = jnp.where(
            sub < 3, p, jnp.where(sub < 6, pltpu.roll(c, 3, 0), pltpu.roll(d, 6, 0))
        )
        return 0

    lax.fori_loop(0, nx, pack, 0, unroll=4)
    pl.semaphore_wait(barrier, 4)

    def remote(a, b, send, recv, k, to):
        copy = pltpu.make_async_remote_copy(
            src_ref=a, dst_ref=b, send_sem=send.at[k], recv_sem=recv.at[k],
            device_id=to, device_id_type=MESH,
        )
        copy.start()
        return copy

    def y_sends(low, high, into_low, into_high, send, recv, k, width, count, head):
        out = []
        tail = head + count
        for dy, part, into in ((1, low, into_low), (-1, high, into_high)):
            out.append(remote(
                part.at[0:width], into.at[tail : tail + width], send, recv, k, device(-1, dy)))
            out.append(remote(
                part.at[count - width : count], into.at[head - width : head],
                send, recv, k + 1, device(1, dy)))
            out.append(remote(part, into.at[head:tail], send, recv, k + 2, device(0, dy)))
            k += 3
        return out

    got = ((got_lo, msg_lo, 1), (got_hi, msg_hi, -1))
    beside_y = [
        remote(msg, into.at[x0:x1], s1, r1, k, device(0, dy)) for k, (into, msg, dy) in enumerate(got)
    ]
    beside_x = []
    k = 2
    for ref, width in ((pot, 3), (cor, 3), (den, 2)):
        beside_x.append(remote(
            ref.at[x1 - width : x1, 0:ny], ref.at[x0 - width : x0, 0:ny], s1, r1, k, device(1, 0)))
        beside_x.append(remote(
            ref.at[x0 : x0 + width, 0:ny], ref.at[x1 : x1 + width, 0:ny], s1, r1, k + 1, device(-1, 0)))
        k += 2

    rows_at = lax.broadcasted_iota(jnp.int32, (4 * nz, nz), 0)
    cols_at = lax.broadcasted_iota(jnp.int32, (4 * nz, nz), 1)
    group = nz // 4
    mean_table = jnp.where(
        (rows_at // nz) * group + (rows_at % nz) // 4 == cols_at, 1.0 / 64.0, 0.0
    ).astype(jnp.bfloat16)

    def pooled(ref, count):
        parts = []
        for y in range(4):
            total = ref[pl.ds(4 * y, count, stride=ny), :]
            for j in range(1, 4):
                total = total + ref[pl.ds(4 * y + j, count, stride=ny), :]
            parts.append(total)
        return dot_exact(jnp.concatenate(parts, axis=1), mean_table)

    for copy in beside_y:
        copy.wait_recv()
    for into in (got_lo, got_hi):
        beside_x.append(remote(
            into.at[x1 - 3 : x1], into.at[1:x0], s1, r1, k, device(1, 0)))
        beside_x.append(remote(
            into.at[x0 : x0 + 3], into.at[x1 : x1 + 3], s1, r1, k + 1, device(-1, 0)))
        k += 2
    round_1 = beside_y + beside_x

    def unpack(at, _):
        lo, hi = got_lo[at], got_hi[at]
        pot[at, ny : ny + 8] = jnp.where(sub < 4, hi, lo)
        cor[at, ny : ny + 8] = jnp.where(sub < 4, pltpu.roll(hi, 5, 0), pltpu.roll(lo, 3, 0))
        den[at, ny : ny + 8] = jnp.where(sub < 4, pltpu.roll(hi, 2, 0), pltpu.roll(lo, 6, 0))
        return 0

    lax.fori_loop(x0, x1, unpack, 0, unroll=4)

    def build(at, v, xs, ys, zs, dxy, dxz, dyz):
        twice = 2.0 * v
        xx, yy, zz = 1.0 + (xs - twice), 1.0 + (ys - twice), 1.0 + (zs - twice)
        xy, xz, yz = 0.25 * dxy, 0.25 * dxz, 0.25 * dyz
        cxx = yy * zz - yz * yz
        cyy = xx * zz - xz * xz
        czz = xx * yy - xy * xy
        cxy = xz * yz - xy * zz
        cxz = xy * yz - xz * yy
        cyz = xy * xz - xx * yz
        src[at] = den[at] - (xx * cxx + xy * cxy + xz * cxz)
        wgt[at] = DAMP / (-2.0 * (cxx + cyy + czz) - SCREEN)
        coef[0, at], coef[1, at], coef[2, at] = cxx, cyy, czz
        coef[3, at], coef[4, at], coef[5, at] = 0.5 * cxy, 0.5 * cxz, 0.5 * cyz

    def off_diagonal(at, xs, ys, zs, dxy, dxz, dyz):
        return (
            (coef[0, at] * xs + coef[1, at] * ys + coef[2, at] * zs)
            + (coef[3, at] * dxy + coef[4, at] * dxz + coef[5, at] * dyz)
        )

    def sweep(a, b, low, high):
        def emit(at, v, *terms):
            b[at] = (1.0 - DAMP) * v + wgt[at] * (src[at] - off_diagonal(at, *terms))

        walk(a, low, high, emit)

    def pool_coef(i, _):
        for f in range(6):
            total = coef[f, x0 + 4 * i, 0:ny]
            for j in range(1, 4):
                total = total + coef[f, x0 + 4 * i + j, 0:ny]
            at = (f * 8 + i) * ny
            pool_c[pl.ds(at if isinstance(i, int) else pl.multiple_of(at, 8), ny), :] = total
        return 0

    walk(pot, x0 + 1, x1 - 1, build)
    sweep(cor, one, x0 + 2, x1 - 2)
    lax.fori_loop(1, nx // 4 - 1, pool_coef, 0, unroll=2)
    for copy in beside_x:
        copy.wait_recv()
    lax.fori_loop(1, x0, unpack, 0, unroll=3)
    lax.fori_loop(x1, x1 + 3, unpack, 0, unroll=3)
    walk(pot, x0 - 2, x0 + 1, build)
    walk(pot, x1 - 1, x1 + 2, build)

    pool_coef(0, 0)
    pool_coef(nx // 4 - 1, 0)
    co[...] = pooled(pool_c, 48).reshape(6, 8, nz)
    for p in range(3):
        f, g = co[2 * p], co[2 * p + 1]
        co_lo[p] = jnp.where(sub < 4, pltpu.roll(f, 6, 0), pltpu.roll(g, 2, 0))
        co_hi[p] = jnp.where(sub < 4, f, pltpu.roll(g, 4, 0))
    coarse_c = []
    for k in (1, 6, 0, 2, 5, 7, 3, 4):
        dx = NEIGHBOURS[k][0]
        if dx == 0:
            a, b = co, got_co.at[(7 - k) - 3]
        else:
            a, b = (co_lo if dx > 0 else co_hi), got_cox.at[7 - k]
        coarse_c.append(remote(a, b, sc, rc, k, device(*NEIGHBOURS[k])))

    def residual_at(at, v, *terms):
        n = ny
        cut = [t[0:n] for t in terms]
        c = [coef[f, at, 0:n] for f in range(6)]
        main = -2.0 * (c[0] + c[1] + c[2]) - SCREEN
        total = c[0] * cut[0] + c[1] * cut[1] + c[2] * cut[2]
        total = total + (c[3] * cut[3] + c[4] * cut[4] + c[5] * cut[5])
        return src[at, 0:n] - (total + main * v[0:n])

    sweep(cor, one, x0 - 2, x0 + 2)
    sweep(cor, one, x1 - 2, x1 + 2)
    sweep(one, two, x0 - 1, x1 + 1)

    def emit_first(at, v, *terms):
        res_out[at - x0] = residual_at(at, v, *terms)

    walk(two, x0, x1, emit_first)
    for i in range(nx // 4):
        pool_s[i * ny : (i + 1) * ny, :] = (
            (res_out[4 * i] + res_out[4 * i + 1]) + (res_out[4 * i + 2] + res_out[4 * i + 3])
        )
    cs[...] = pooled(pool_s, 8)
    coarse_s = [
        remote(cs, got_cs.at[7 - k], ss, rs, k, device(*NEIGHBOURS[k]))
        for k in (0, 2, 5, 7, 1, 6, 3, 4)
    ]

    round_2 = [
        remote(two.at[x1 - 3 : x1, 0:ny], fin.at[1:x0, 0:ny], s2, r2, 0, device(1, 0)),
        remote(two.at[x0 : x0 + 3, 0:ny], fin.at[x1 : x1 + 3, 0:ny], s2, r2, 1, device(-1, 0)),
    ]
    for q in range(nx // 2):
        a, b = x0 + 2 * q, x0 + 2 * q + 1
        out_lo[q] = jnp.where(sub < 4, pltpu.roll(two[a, ny - 8 : ny], 4, 0), two[b, ny - 8 : ny])
        out_hi[q] = jnp.where(sub < 4, two[a, 0:8], pltpu.roll(two[b, 0:8], 4, 0))
    round_2 += y_sends(out_lo, out_hi, est_lo, est_hi, s2, r2, 2, 2, nx // 2, x0 // 2)

    def place(field, at_y, dx, value):
        if dx < 0:
            wide[field, at_y, 0:4, :] = value[2:6]
        elif dx == 0:
            wide[field, at_y, 4:10, :] = value[0:6]
        else:
            wide[field, at_y, 10:14, :] = value[0:4]

    rows_b = lax.broadcasted_iota(jnp.int32, (nz, nz), 0)
    cols_b = lax.broadcasted_iota(jnp.int32, (nz, nz), 1)
    for g in range(4):
        back[g] = jnp.where(rows_b == g * group + cols_b // 4, 1.0, 0.0).astype(jnp.bfloat16)
    for f in range(6):
        place(f, 1, 0, co[f])
    place(6, 1, 0, cs[...])
    for copy in coarse_c:
        copy.wait_recv()
    for k, (dx, dy) in enumerate(NEIGHBOURS):
        for f in range(6):
            if dx == 0:
                place(f, dy + 1, 0, got_co[k - 3, f])
            else:
                row_at, part = (0 if dx < 0 else 10), 4 * (f % 2)
                wide[f, dy + 1, row_at : row_at + 4, :] = got_cox[k, f // 2, part : part + 4]
    cc = [wide[f] for f in range(6)]
    spacing = 1.0 / 16.0
    coarse_w = DAMP / (-2.0 * spacing * (cc[0] + cc[1] + cc[2]) - SCREEN)
    cc = [spacing * c for c in cc]
    for copy in coarse_s:
        copy.wait_recv()
    for k, (dx, dy) in enumerate(NEIGHBOURS):
        place(6, dy + 1, dx, got_cs[k])
    coarse_b = wide[6]
    lane = lax.broadcasted_iota(jnp.int32, (3, 16, nz), 2)
    in_group = lane % group

    def y_up(v):
        r = pltpu.roll(v, nz - group, 2)
        return jnp.where(lane < nz - group, r, jnp.concatenate([r[1:], r[:1]], axis=0))

    def y_down(v):
        r = pltpu.roll(v, group, 2)
        return jnp.where(lane >= group, r, jnp.concatenate([r[2:], r[:2]], axis=0))

    value = coarse_w * coarse_b
    for _ in range(3):
        zp = jnp.where(in_group == group - 1, pltpu.roll(value, group - 1, 2), pltpu.roll(value, nz - 1, 2))
        zm = jnp.where(in_group == 0, pltpu.roll(value, nz - group + 1, 2), pltpu.roll(value, 1, 2))
        dz = zp - zm
        yp, ym = y_up(value), y_down(value)
        dy_ = yp - ym
        xs = pltpu.roll(value, 15, 1) + pltpu.roll(value, 1, 1)
        dxy = pltpu.roll(dy_, 15, 1) - pltpu.roll(dy_, 1, 1)
        dxz = pltpu.roll(dz, 15, 1) - pltpu.roll(dz, 1, 1)
        dyz = y_up(dz) - y_down(dz)
        total = cc[0] * xs + cc[1] * (yp + ym) + cc[2] * (zp + zm)
        total = total + (cc[3] * dxy + cc[4] * dxz + cc[5] * dyz)
        value = (1.0 - DAMP) * value + coarse_w * (coarse_b - total)

    for j, (blk, g) in enumerate(((0, 3), (1, 0), (1, 1), (1, 2), (1, 3), (2, 0))):
        grown[j] = dot_exact(value[blk], back[g])

    for copy in round_2:
        copy.wait_recv()

    def row(j, i):
        return jnp.broadcast_to(grown[j, 3 + i : 4 + i, :], (8, nz))

    for i in range(nx // 4 + 2):
        a0 = jnp.where(sub < 4, row(1, i), row(2, i))
        a1 = jnp.where(sub < 4, row(3, i), row(4, i))
        a2 = jnp.where(sub < 4, row(5, i), row(0, i))
        for at in range(4 * i, 4 * i + 4):
            if 1 <= at < x1 + 3:
                base = two if x0 <= at < x1 else fin
                fin[at, 0:8] = base[at, 0:8] + a0
                fin[at, 8:16] = base[at, 8:16] + a1
                lo, hi = est_lo[at // 2], est_hi[at // 2]
                if at % 2 == 0:
                    lo = pltpu.roll(lo, 4, 0)
                else:
                    hi = pltpu.roll(hi, 4, 0)
                fin[at, ny : ny + 8] = jnp.where(sub < 4, hi, lo) + a2

    sweep(fin, one, x0 - 2, x1 + 2)
    for copy in round_2:
        copy.wait_send()
    sweep(one, two, x0 - 1, x1 + 1)

    def emit_last(at, v, *terms):
        up_out[at - x0] = 0.5 * v[0:ny]
        res_out[at - x0] = 0.5 * residual_at(at, v, *terms)

    walk(two, x0, x1, emit_last)
    for copy in round_1 + coarse_c + coarse_s:
        copy.wait_send()


def solution(mesh):
    gx_n, gy_n = mesh.shape["gx"], mesh.shape["gy"]

    def shards(potential, density, correction):
        nx, ny, nz = potential.shape
        fine = pltpu.VMEM((nx + 8, ny + 8, nz), F32)
        side = pltpu.VMEM((nx + 8, 8, nz), F32)
        half_out = pltpu.VMEM((nx // 2, 8, nz), F32)
        half = pltpu.VMEM((nx // 2 + 4, 8, nz), F32)
        dma = pltpu.SemaphoreType.DMA
        shape = jax.ShapeDtypeStruct(potential.shape, F32)
        updated, residual = pl.pallas_call(
            functools.partial(kernel, gx_n, gy_n),
            out_shape=(shape, shape),
            in_specs=[pl.BlockSpec(memory_space=pl.ANY)] * 3,
            out_specs=[pl.BlockSpec(memory_space=pltpu.VMEM)] * 2,
            scratch_shapes=[
                fine, fine, fine,
                pltpu.VMEM((6, nx + 8, ny + 8, nz), F32),
                fine, fine, fine, fine, fine,
                pltpu.VMEM((nx, 8, nz), F32), pltpu.VMEM((nx, 8, nz), F32),
                side, side, half_out, half_out, half, half,
                pltpu.VMEM((48 * ny, nz), F32), pltpu.VMEM((8 * ny, nz), F32),
                pltpu.VMEM((6, 8, nz), F32), pltpu.VMEM((3, 8, nz), F32), pltpu.VMEM((3, 8, nz), F32),
                pltpu.VMEM((8, nz), F32),
                pltpu.VMEM((2, 6, 8, nz), F32), pltpu.VMEM((8, 3, 8, nz), F32), pltpu.VMEM((8, 8, nz), F32),
                pltpu.VMEM((7, 3, 16, nz), F32), pltpu.VMEM((6, 16, nz), F32),
                pltpu.VMEM((4, nz, nz), jnp.bfloat16),
                dma((3,)), dma((12,)), dma((12,)), dma((8,)), dma((8,)),
                dma((8,)), dma((8,)), dma((8,)), dma((8,)),
            ],
            compiler_params=pltpu.CompilerParams(
                collective_id=0, has_side_effects=True, vmem_limit_bytes=40 * 1024 * 1024
            ),
        )(*[
            pltpu.with_memory_space_constraint(v, pltpu.HBM) for v in (potential, density, correction)
        ])
        return 2.0 * updated, 2.0 * residual

    placed = (P("gx", "gy", None),) * 3
    return jax.shard_map(
        shards, mesh=mesh, in_specs=placed,
        out_specs=(P("gx", "gy", None), P("gx", "gy", None)), check_vma=False,
    )
```

```python
import functools

import jax
import jax.numpy as jnp
from jax import lax
from jax.experimental import pallas as pl
from jax.experimental.pallas import tpu as pltpu
from jax.sharding import PartitionSpec as P

MESH = pl.DeviceIdType.MESH
SCREEN = 0.002
DAMP = 0.6
UNROLL = {3: 3, 4: 4, 20: 10, 22: 11, 24: 12, 26: 13, 28: 14}
F32 = jnp.float32
BESIDE = [(-1, 0), (1, 0), (0, -1), (0, 1)]
NEIGHBOURS = [(-1, -1), (-1, 0), (-1, 1), (0, -1), (0, 1), (1, -1), (1, 0), (1, 1)]


def first_plane(ref, at):
    v = ref[at]
    rows = v.shape[0]
    zp = pltpu.roll(v, v.shape[1] - 1, 1)
    zm = pltpu.roll(v, 1, 1)
    yp = pltpu.roll(v, rows - 1, 0)
    ym = pltpu.roll(v, 1, 0)
    dz = zp - zm
    dyz = pltpu.roll(dz, rows - 1, 0) - pltpu.roll(dz, 1, 0)
    return v, dz, yp - ym, zp + zm, yp + ym, dyz


def walk(ref, low, high, emit):
    def step(at, carry):
        before, here = carry
        after = first_plane(ref, at + 1)
        emit(
            at,
            here[0],
            before[0] + after[0],
            here[4],
            here[3],
            after[2] - before[2],
            after[1] - before[1],
            here[5],
        )
        return here[:3], after

    start = (first_plane(ref, low - 1)[:3], first_plane(ref, low))
    lax.fori_loop(low, high, step, start, unroll=UNROLL.get(high - low, 7))


def dot_exact(values, table):
    hi = values.astype(jnp.bfloat16)
    rest = values - hi.astype(F32)
    mid = rest.astype(jnp.bfloat16)
    lo = (rest - mid.astype(F32)).astype(jnp.bfloat16)
    n = values.shape[0]
    out = jnp.dot(jnp.concatenate([hi, mid, lo], axis=0), table, preferred_element_type=F32)
    return out[:n] + out[n : 2 * n] + out[2 * n :]


def kernel(
    gx_n, gy_n, p_in, d_in, c_in, up_out, res_out,
    pot, cor, den, coef, wgt, src, one, two, fin,
    msg_lo, msg_hi, got_lo, got_hi, out_lo, out_hi, est_lo, est_hi,
    pool_c, pool_s, co, co_lo, co_hi, cs, got_co, got_cox, got_cs, wide, grown, back,
    in_sem, s1, r1, s2, r2, sc, rc, ss, rs,
):
    nx, ny, nz = p_in.shape
    x0, x1 = 4, 4 + nx
    gx = lax.axis_index("gx")
    gy = lax.axis_index("gy")

    def device(dx, dy):
        return (lax.rem(gx + dx + gx_n, gx_n), lax.rem(gy + dy + gy_n, gy_n))

    barrier = pltpu.get_barrier_semaphore()
    for dx, dy in BESIDE:
        pl.semaphore_signal(barrier, inc=1, device_id=device(dx, dy), device_id_type=MESH)
    loads = []
    for k, (a, b) in enumerate(((p_in, pot), (c_in, cor), (d_in, den))):
        copy = pltpu.make_async_copy(a, b.at[x0:x1, 0:ny], in_sem.at[k])
        copy.start()
        loads.append(copy)
    sub = lax.broadcasted_iota(jnp.int32, (8, nz), 0)
    wide[:, :, 14:16, :] = jnp.zeros((7, 3, 2, nz), F32)
    for f in range(6):
        pool_c[(f * 8 + 6) * ny : (f * 8 + 8) * ny, :] = jnp.zeros((2 * ny, nz), F32)
    pool_s[6 * ny : 8 * ny, :] = jnp.zeros((2 * ny, nz), F32)

    for copy in loads:
        copy.wait()

    def pack(x, _):
        top = ny - 8
        p, c, d = pot[x0 + x, top:ny], cor[x0 + x, top:ny], den[x0 + x, top:ny]
        msg_lo[x] = jnp.where(
            sub >= 5, p, jnp.where(sub >= 2, pltpu.roll(c, 5, 0), pltpu.roll(d, 2, 0))
        )
        p, c, d = pot[x0 + x, 0:8], cor[x0 + x, 0:8], den[x0 + x, 0:8]
        msg_hi[x] = jnp.where(
            sub < 3, p, jnp.where(sub < 6, pltpu.roll(c, 3, 0), pltpu.roll(d, 6, 0))
        )
        return 0

    lax.fori_loop(0, nx, pack, 0, unroll=4)
    pl.semaphore_wait(barrier, 4)

    def remote(a, b, send, recv, k, to):
        copy = pltpu.make_async_remote_copy(
            src_ref=a, dst_ref=b, send_sem=send.at[k], recv_sem=recv.at[k],
            device_id=to, device_id_type=MESH,
        )
        copy.start()
        return copy

    def y_sends(low, high, into_low, into_high, send, recv, k, width, count, head):
        out = []
        tail = head + count
        for dy, part, into in ((1, low, into_low), (-1, high, into_high)):
            out.append(remote(
                part.at[0:width], into.at[tail : tail + width], send, recv, k, device(-1, dy)))
            out.append(remote(
                part.at[count - width : count], into.at[head - width : head],
                send, recv, k + 1, device(1, dy)))
            out.append(remote(part, into.at[head:tail], send, recv, k + 2, device(0, dy)))
            k += 3
        return out

    got = ((got_lo, msg_lo, 1), (got_hi, msg_hi, -1))
    beside_y = [
        remote(msg, into.at[x0:x1], s1, r1, k, device(0, dy)) for k, (into, msg, dy) in enumerate(got)
    ]
    beside_x = []
    k = 2
    for ref, width in ((pot, 3), (cor, 3), (den, 2)):
        beside_x.append(remote(
            ref.at[x1 - width : x1, 0:ny], ref.at[x0 - width : x0, 0:ny], s1, r1, k, device(1, 0)))
        beside_x.append(remote(
            ref.at[x0 : x0 + width, 0:ny], ref.at[x1 : x1 + width, 0:ny], s1, r1, k + 1, device(-1, 0)))
        k += 2

    rows_at = lax.broadcasted_iota(jnp.int32, (4 * nz, nz), 0)
    cols_at = lax.broadcasted_iota(jnp.int32, (4 * nz, nz), 1)
    group = nz // 4
    mean_table = jnp.where(
        (rows_at // nz) * group + (rows_at % nz) // 4 == cols_at, 1.0 / 64.0, 0.0
    ).astype(jnp.bfloat16)

    def pooled(ref, count):
        parts = []
        for y in range(4):
            total = ref[pl.ds(4 * y, count, stride=ny), :]
            for j in range(1, 4):
                total = total + ref[pl.ds(4 * y + j, count, stride=ny), :]
            parts.append(total)
        return dot_exact(jnp.concatenate(parts, axis=1), mean_table)

    for copy in beside_y:
        copy.wait_recv()
    for into in (got_lo, got_hi):
        beside_x.append(remote(
            into.at[x1 - 3 : x1], into.at[1:x0], s1, r1, k, device(1, 0)))
        beside_x.append(remote(
            into.at[x0 : x0 + 3], into.at[x1 : x1 + 3], s1, r1, k + 1, device(-1, 0)))
        k += 2
    round_1 = beside_y + beside_x

    def unpack(at, _):
        lo, hi = got_lo[at], got_hi[at]
        pot[at, ny : ny + 8] = jnp.where(sub < 4, hi, lo)
        cor[at, ny : ny + 8] = jnp.where(sub < 4, pltpu.roll(hi, 5, 0), pltpu.roll(lo, 3, 0))
        den[at, ny : ny + 8] = jnp.where(sub < 4, pltpu.roll(hi, 2, 0), pltpu.roll(lo, 6, 0))
        return 0

    lax.fori_loop(x0, x1, unpack, 0, unroll=4)

    def build(at, v, xs, ys, zs, dxy, dxz, dyz):
        twice = 2.0 * v
        xx, yy, zz = 1.0 + (xs - twice), 1.0 + (ys - twice), 1.0 + (zs - twice)
        xy, xz, yz = 0.25 * dxy, 0.25 * dxz, 0.25 * dyz
        cxx = yy * zz - yz * yz
        cyy = xx * zz - xz * xz
        czz = xx * yy - xy * xy
        cxy = xz * yz - xy * zz
        cxz = xy * yz - xz * yy
        cyz = xy * xz - xx * yz
        src[at] = den[at] - (xx * cxx + xy * cxy + xz * cxz)
        wgt[at] = DAMP / (-2.0 * (cxx + cyy + czz) - SCREEN)
        coef[0, at], coef[1, at], coef[2, at] = cxx, cyy, czz
        coef[3, at], coef[4, at], coef[5, at] = 0.5 * cxy, 0.5 * cxz, 0.5 * cyz

    def off_diagonal(at, xs, ys, zs, dxy, dxz, dyz):
        return (
            (coef[0, at] * xs + coef[1, at] * ys + coef[2, at] * zs)
            + (coef[3, at] * dxy + coef[4, at] * dxz + coef[5, at] * dyz)
        )

    def sweep(a, b, low, high):
        def emit(at, v, *terms):
            b[at] = (1.0 - DAMP) * v + wgt[at] * (src[at] - off_diagonal(at, *terms))

        walk(a, low, high, emit)

    def pool_coef(i, _):
        for f in range(6):
            total = coef[f, x0 + 4 * i, 0:ny]
            for j in range(1, 4):
                total = total + coef[f, x0 + 4 * i + j, 0:ny]
            at = (f * 8 + i) * ny
            pool_c[pl.ds(at if isinstance(i, int) else pl.multiple_of(at, 8), ny), :] = total
        return 0

    walk(pot, x0 + 1, x1 - 1, build)
    sweep(cor, one, x0 + 2, x1 - 2)
    lax.fori_loop(1, nx // 4 - 1, pool_coef, 0, unroll=2)
    for copy in beside_x:
        copy.wait_recv()
    lax.fori_loop(1, x0, unpack, 0, unroll=3)
    lax.fori_loop(x1, x1 + 3, unpack, 0, unroll=3)
    walk(pot, x0 - 2, x0 + 1, build)
    walk(pot, x1 - 1, x1 + 2, build)

    pool_coef(0, 0)
    pool_coef(nx // 4 - 1, 0)
    co[...] = pooled(pool_c, 48).reshape(6, 8, nz)
    for p in range(3):
        f, g = co[2 * p], co[2 * p + 1]
        co_lo[p] = jnp.where(sub < 4, pltpu.roll(f, 6, 0), pltpu.roll(g, 2, 0))
        co_hi[p] = jnp.where(sub < 4, f, pltpu.roll(g, 4, 0))
    coarse_c = []
    for k in (1, 6, 0, 2, 5, 7, 3, 4):
        dx = NEIGHBOURS[k][0]
        if dx == 0:
            a, b = co, got_co.at[(7 - k) - 3]
        else:
            a, b = (co_lo if dx > 0 else co_hi), got_cox.at[7 - k]
        coarse_c.append(remote(a, b, sc, rc, k, device(*NEIGHBOURS[k])))

    def residual_at(at, v, *terms):
        n = ny
        cut = [t[0:n] for t in terms]
        c = [coef[f, at, 0:n] for f in range(6)]
        main = -2.0 * (c[0] + c[1] + c[2]) - SCREEN
        total = c[0] * cut[0] + c[1] * cut[1] + c[2] * cut[2]
        total = total + (c[3] * cut[3] + c[4] * cut[4] + c[5] * cut[5])
        return src[at, 0:n] - (total + main * v[0:n])

    sweep(cor, one, x0 - 2, x0 + 2)
    sweep(cor, one, x1 - 2, x1 + 2)
    sweep(one, two, x0 - 1, x1 + 1)

    def emit_first(at, v, *terms):
        res_out[at - x0] = residual_at(at, v, *terms)

    walk(two, x0, x1, emit_first)
    for i in range(nx // 4):
        pool_s[i * ny : (i + 1) * ny, :] = (
            (res_out[4 * i] + res_out[4 * i + 1]) + (res_out[4 * i + 2] + res_out[4 * i + 3])
        )
    cs[...] = pooled(pool_s, 8)
    coarse_s = [
        remote(cs, got_cs.at[7 - k], ss, rs, k, device(*NEIGHBOURS[k]))
        for k in (0, 2, 5, 7, 1, 6, 3, 4)
    ]

    round_2 = [
        remote(two.at[x1 - 3 : x1, 0:ny], fin.at[1:x0, 0:ny], s2, r2, 0, device(1, 0)),
        remote(two.at[x0 : x0 + 3, 0:ny], fin.at[x1 : x1 + 3, 0:ny], s2, r2, 1, device(-1, 0)),
    ]
    for q in range(nx // 2):
        a, b = x0 + 2 * q, x0 + 2 * q + 1
        out_lo[q] = jnp.where(sub < 4, pltpu.roll(two[a, ny - 8 : ny], 4, 0), two[b, ny - 8 : ny])
        out_hi[q] = jnp.where(sub < 4, two[a, 0:8], pltpu.roll(two[b, 0:8], 4, 0))
    round_2 += y_sends(out_lo, out_hi, est_lo, est_hi, s2, r2, 2, 2, nx // 2, x0 // 2)

    def place(field, at_y, dx, value):
        if dx < 0:
            wide[field, at_y, 0:4, :] = value[2:6]
        elif dx == 0:
            wide[field, at_y, 4:10, :] = value[0:6]
        else:
            wide[field, at_y, 10:14, :] = value[0:4]

    rows_b = lax.broadcasted_iota(jnp.int32, (nz, nz), 0)
    cols_b = lax.broadcasted_iota(jnp.int32, (nz, nz), 1)
    for g in range(4):
        back[g] = jnp.where(rows_b == g * group + cols_b // 4, 1.0, 0.0).astype(jnp.bfloat16)
    for f in range(6):
        place(f, 1, 0, co[f])
    place(6, 1, 0, cs[...])
    for copy in coarse_c:
        copy.wait_recv()
    for k, (dx, dy) in enumerate(NEIGHBOURS):
        for f in range(6):
            if dx == 0:
                place(f, dy + 1, 0, got_co[k - 3, f])
            else:
                row_at, part = (0 if dx < 0 else 10), 4 * (f % 2)
                wide[f, dy + 1, row_at : row_at + 4, :] = got_cox[k, f // 2, part : part + 4]
    cc = [wide[f] for f in range(6)]
    spacing = 1.0 / 16.0
    coarse_w = DAMP / (-2.0 * spacing * (cc[0] + cc[1] + cc[2]) - SCREEN)
    cc = [spacing * c for c in cc]
    for copy in coarse_s:
        copy.wait_recv()
    for k, (dx, dy) in enumerate(NEIGHBOURS):
        place(6, dy + 1, dx, got_cs[k])
    coarse_b = wide[6]
    lane = lax.broadcasted_iota(jnp.int32, (3, 16, nz), 2)
    in_group = lane % group

    def y_up(v):
        r = pltpu.roll(v, nz - group, 2)
        return jnp.where(lane < nz - group, r, jnp.concatenate([r[1:], r[:1]], axis=0))

    def y_down(v):
        r = pltpu.roll(v, group, 2)
        return jnp.where(lane >= group, r, jnp.concatenate([r[2:], r[:2]], axis=0))

    value = coarse_w * coarse_b
    for _ in range(3):
        zp = jnp.where(in_group == group - 1, pltpu.roll(value, group - 1, 2), pltpu.roll(value, nz - 1, 2))
        zm = jnp.where(in_group == 0, pltpu.roll(value, nz - group + 1, 2), pltpu.roll(value, 1, 2))
        dz = zp - zm
        yp, ym = y_up(value), y_down(value)
        dy_ = yp - ym
        xs = pltpu.roll(value, 15, 1) + pltpu.roll(value, 1, 1)
        dxy = pltpu.roll(dy_, 15, 1) - pltpu.roll(dy_, 1, 1)
        dxz = pltpu.roll(dz, 15, 1) - pltpu.roll(dz, 1, 1)
        dyz = y_up(dz) - y_down(dz)
        total = cc[0] * xs + cc[1] * (yp + ym) + cc[2] * (zp + zm)
        total = total + (cc[3] * dxy + cc[4] * dxz + cc[5] * dyz)
        value = (1.0 - DAMP) * value + coarse_w * (coarse_b - total)

    for j, (blk, g) in enumerate(((0, 3), (1, 0), (1, 1), (1, 2), (1, 3), (2, 0))):
        grown[j] = dot_exact(value[blk], back[g])

    def row(j, i):
        return jnp.broadcast_to(grown[j, 3 + i : 4 + i, :], (8, nz))

    def add_own_rows(i, base):
        a0 = jnp.where(sub < 4, row(1, i), row(2, i))
        a1 = jnp.where(sub < 4, row(3, i), row(4, i))
        for at in range(max(4 * i, 1), min(4 * i + 4, x1 + 3)):
            fin[at, 0:8] = base[at, 0:8] + a0
            fin[at, 8:16] = base[at, 8:16] + a1

    for i in range(1, nx // 4 + 1):
        add_own_rows(i, two)
    for copy in round_2:
        copy.wait_recv()
    add_own_rows(0, fin)
    add_own_rows(nx // 4 + 1, fin)
    for i in range(nx // 4 + 2):
        a2 = jnp.where(sub < 4, row(5, i), row(0, i))
        for at in range(max(4 * i, 1), min(4 * i + 4, x1 + 3)):
            lo, hi = est_lo[at // 2], est_hi[at // 2]
            if at % 2 == 0:
                lo = pltpu.roll(lo, 4, 0)
            else:
                hi = pltpu.roll(hi, 4, 0)
            fin[at, ny : ny + 8] = jnp.where(sub < 4, hi, lo) + a2

    sweep(fin, one, x0 - 2, x1 + 2)
    for copy in round_2:
        copy.wait_send()
    sweep(one, two, x0 - 1, x1 + 1)

    def emit_last(at, v, *terms):
        up_out[at - x0] = 0.5 * v[0:ny]
        res_out[at - x0] = 0.5 * residual_at(at, v, *terms)

    walk(two, x0, x1, emit_last)
    for copy in round_1 + coarse_c + coarse_s:
        copy.wait_send()


def solution(mesh):
    gx_n, gy_n = mesh.shape["gx"], mesh.shape["gy"]

    def shards(potential, density, correction):
        nx, ny, nz = potential.shape
        fine = pltpu.VMEM((nx + 8, ny + 8, nz), F32)
        side = pltpu.VMEM((nx + 8, 8, nz), F32)
        half_out = pltpu.VMEM((nx // 2, 8, nz), F32)
        half = pltpu.VMEM((nx // 2 + 4, 8, nz), F32)
        dma = pltpu.SemaphoreType.DMA
        shape = jax.ShapeDtypeStruct(potential.shape, F32)
        updated, residual = pl.pallas_call(
            functools.partial(kernel, gx_n, gy_n),
            out_shape=(shape, shape),
            in_specs=[pl.BlockSpec(memory_space=pl.ANY)] * 3,
            out_specs=[pl.BlockSpec(memory_space=pltpu.VMEM)] * 2,
            scratch_shapes=[
                fine, fine, fine,
                pltpu.VMEM((6, nx + 8, ny + 8, nz), F32),
                fine, fine, fine, fine, fine,
                pltpu.VMEM((nx, 8, nz), F32), pltpu.VMEM((nx, 8, nz), F32),
                side, side, half_out, half_out, half, half,
                pltpu.VMEM((48 * ny, nz), F32), pltpu.VMEM((8 * ny, nz), F32),
                pltpu.VMEM((6, 8, nz), F32), pltpu.VMEM((3, 8, nz), F32), pltpu.VMEM((3, 8, nz), F32),
                pltpu.VMEM((8, nz), F32),
                pltpu.VMEM((2, 6, 8, nz), F32), pltpu.VMEM((8, 3, 8, nz), F32), pltpu.VMEM((8, 8, nz), F32),
                pltpu.VMEM((7, 3, 16, nz), F32), pltpu.VMEM((6, 16, nz), F32),
                pltpu.VMEM((4, nz, nz), jnp.bfloat16),
                dma((3,)), dma((12,)), dma((12,)), dma((8,)), dma((8,)),
                dma((8,)), dma((8,)), dma((8,)), dma((8,)),
            ],
            compiler_params=pltpu.CompilerParams(
                collective_id=0, has_side_effects=True, vmem_limit_bytes=40 * 1024 * 1024
            ),
        )(*[
            pltpu.with_memory_space_constraint(v, pltpu.HBM) for v in (potential, density, correction)
        ])
        return 2.0 * updated, 2.0 * residual

    placed = (P("gx", "gy", None),) * 3
    return jax.shard_map(
        shards, mesh=mesh, in_specs=placed,
        out_specs=(P("gx", "gy", None), P("gx", "gy", None)), check_vma=False,
    )
```
